32 devices in a mesh: row: 8 (over y, x, core), col: 4 (over z).
Axes of the slice: x: 2, y: 2, z: 4, core: 2. Of those that a mesh axis runs over, the one named last changes fastest.
Arguments:
- matrix: float32 [16384, 16384], P('row', 'col'), may hold values from -80 to 80
Outputs:
- reduced: float32 [16384, 16384], P('row', 'col')
The draws below stay inside these ranges and needn't reach their ends.
All inputs are finite; a program needn't handle non-finite values.
Results may differ from the reference program's by a relative error of at most 0.0003.
Values sent between devices are 32-bit elements; how exact they have to be, the bound alone decides.
A program may use at most 128 MiB of HBM per device.

```python
import jax
import jax.numpy as jnp
from jax import lax

ORDER = 16384
B = 64
PANELS = 1


def draw_matrix(key, part):
    first_key = jax.random.fold_in(key, 11)
    base = jax.random.truncated_normal(first_key, -6.0, 6.0, (ORDER, ORDER), jnp.float32)
    symmetric = (base + base.T) * jnp.float32(0.5 ** 0.5)
    return symmetric


def setup_inputs(seed: int = 0) -> dict:
    key_list = jax.random.split(jax.random.key(seed), 2)
    matrix = draw_matrix(jax.random.fold_in(key_list[1], 71), 0)
    return {"matrix": matrix}


def product(left, right):
    return jnp.dot(left.astype(jnp.float32), right.astype(jnp.float32), precision=lax.Precision.HIGHEST, preferred_element_type=jnp.float32)

def sign_lu(block):
    work = block
    count = block.shape[0]
    unit_lower = jnp.eye(count, dtype=block.dtype)
    signs = []
    for column in range(count):
        pivot = work[column, column]
        sign_value = jnp.where(pivot >= 0, -jnp.ones_like(pivot), jnp.ones_like(pivot))
        work = work.at[column, column].add(-sign_value)
        below = work[column + 1:, column] / work[column, column]
        unit_lower = unit_lower.at[column + 1:, column].set(below)
        work = work.at[column + 1:, column + 1:].add(-below[:, None] * work[column, column + 1:][None, :])
        signs.append(sign_value)
    return (unit_lower, jnp.triu(work), jnp.stack(signs))

def reference(matrix):
    current = matrix
    indices = jnp.arange(ORDER, dtype=jnp.int32)
    identity = jnp.eye(B, dtype=matrix.dtype)
    for panel_index in range(PANELS):
        first = panel_index * B
        limit = first + B
        panel = jnp.where(indices[:, None] >= limit, current[:, first:limit], jnp.zeros_like(current[:, first:limit]))
        gram_matrix = product(panel.T, panel)
        lower_factor = jnp.linalg.cholesky(gram_matrix)
        basis = jax.scipy.linalg.solve_triangular(lower_factor, panel.T, lower=True).T
        top_basis = basis[limit:limit + B]
        unit_lower, upper, signs = sign_lu(top_basis)
        inverse_upper = jax.scipy.linalg.solve_triangular(upper, identity, lower=False)
        inverse_lower = jax.scipy.linalg.solve_triangular(unit_lower, identity, lower=True, unit_diagonal=True)
        factor = -product(upper * signs[None, :], inverse_lower.T)
        shifted = signs[:, None] * inverse_upper
        vectors = product(basis, inverse_upper)
        vectors = vectors.at[limit:limit + B].add(-shifted)
        image = product(current, vectors)
        projected = product(vectors.T, image)
        inner = product(factor.T, product(projected, factor))
        update = product(image, factor) - 0.5 * product(vectors, inner)
        current = current - product(vectors, update.T) - product(update, vectors.T)
    return current
```

```python
import jax
import jax.numpy as jnp
from jax import lax
from jax.experimental import pallas as pl
from jax.experimental.pallas import tpu as pltpu
from jax.sharding import PartitionSpec as P

B = 64
STEP = 8


highest = lax.Precision.HIGHEST
MESH = pl.DeviceIdType.MESH
f32 = jnp.float32
bf16 = jnp.bfloat16
NT = (((1,), (1,)), ((), ()))
TN = (((0,), (0,)), ((), ()))


def product(left, right):
    return jnp.dot(left, right, precision=highest, preferred_element_type=f32)


def product_nt(left, right):
    return lax.dot_general(left, right, NT, precision=highest, preferred_element_type=f32)


def product_tn(left, right):
    return lax.dot_general(left, right, TN, precision=highest, preferred_element_type=f32)


def split(x):
    upper = x.astype(bf16)
    return upper, (x - upper.astype(f32)).astype(bf16)


def eliminate(work, rows):
    for j in range(0, B, STEP):
        columns = [jnp.broadcast_to(work[:, j + k : j + k + 1], work.shape) for k in range(STEP)]
        lines = [work[j + k : j + k + 1, :] for k in range(STEP)]
        small = [[columns[c][j + r : j + r + 1, :] for c in range(STEP)] for r in range(STEP)]
        scaled = []
        for k in range(STEP):
            inverse = 1.0 / small[k][k]
            scaled.append(lines[k] * inverse)
            for m in range(k + 1, STEP):
                ratio = small[k][m] * inverse
                columns[m] = columns[m] - columns[k] * ratio
                lines[m] = lines[m] - lines[k] * ratio
                for c in range(m, STEP):
                    small[m][c] = small[m][c] - ratio * small[k][c]
        lowered = work
        for k in range(STEP):
            lowered = lowered - columns[k] * scaled[k]
        lowered = jnp.where(rows >= j + STEP, lowered, work)
        for k in range(1, STEP):
            lowered = jnp.where(rows == j + k, lines[k], lowered)
        work = lowered
    return work


def sign_inverse(q, rows):
    lane = lax.broadcasted_iota(jnp.int32, (1, 2 * B), 1)
    signs = jnp.zeros((B, 2 * B), f32)
    for j in range(0, B, STEP):
        columns = [jnp.broadcast_to(q[:, j + k : j + k + 1], q.shape) for k in range(STEP)]
        lines = [q[j + k : j + k + 1, :] for k in range(STEP)]
        small = [[columns[c][j + r : j + r + 1, :] for c in range(STEP)] for r in range(STEP)]
        scaled = []
        chosen = []
        for k in range(STEP):
            sign = jnp.where(small[k][k] >= 0, f32(-1.0), f32(1.0))
            pivot = small[k][k] - sign
            inverse = 1.0 / pivot
            chosen.append(sign)
            lines[k] = jnp.where(lane == j + k, pivot, lines[k]) * inverse
            scaled.append(lines[k])
            for c in range(k + 1, STEP):
                small[k][c] = small[k][c] * inverse
                columns[c] = columns[c] - columns[k] * small[k][c]
            for r in range(STEP):
                if r != k:
                    lines[r] = lines[r] - small[r][k] * lines[k]
                    for c in range(k + 1, STEP):
                        small[r][c] = small[r][c] - small[r][k] * small[k][c]
        for k in range(STEP):
            q = q - columns[k] * scaled[k]
        for k in range(STEP):
            q = jnp.where(rows == j + k, lines[k], q)
            signs = jnp.where(rows == j + k, chosen[k], signs)
    return q[:, B:], signs[:, :1]


def factor_values(gram, top):
    rows = lax.broadcasted_iota(jnp.int32, (B, 2 * B), 0)
    lanes = lax.broadcasted_iota(jnp.int32, (B, 2 * B), 1)
    small_rows = lax.broadcasted_iota(jnp.int32, (B, B), 0)
    small_lanes = lax.broadcasted_iota(jnp.int32, (B, B), 1)
    eye = jnp.where(small_rows == small_lanes, f32(1.0), f32(0.0))
    work = eliminate(jnp.concatenate([gram, eye], axis=1), rows)
    pivots = jnp.sum(jnp.where(rows == lanes, work, f32(0.0)), axis=1, keepdims=True)
    work = work * (1.0 / jnp.sqrt(pivots))
    upper = jnp.where(small_lanes >= small_rows, work[:, :B], f32(0.0))
    lower_inverse = work[:, B:]
    basis = product_nt(top, lower_inverse)
    inverse, signs = sign_inverse(jnp.concatenate([basis, eye], axis=1), rows)
    factor = -product_tn(lower_inverse, product(signs * inverse.T, lower_inverse))
    return factor, (signs * upper).T


def remote(src, dst, send_sem, recv_sem, device):
    return pltpu.make_async_remote_copy(
        src_ref=src,
        dst_ref=dst,
        send_sem=send_sem,
        recv_sem=recv_sem,
        device_id=device,
        device_id_type=MESH,
    )


def front_kernel(
    height, breadth, matrix, block, left, right,
    slab, strip, pc, pr, halves, own, parts, stats, chained, zs, rs, wr, wc, pe, ps, pt,
    local_sems, block_sems, pc_recvs, ring_sends, mate_sends, pr_recvs, pr_sends, part_sends, part_recvs,
    stat_sends, stat_recv, chain_send, chain_recv, rs_sends, rs_recvs, wr_right, wr_left, wr_recvs,
    role_send, wc_recvs, wc_sends, pe_sends, pe_recvs, pt_sends, pt_recvs,
):
    r, c = lax.axis_index("row"), lax.axis_index("col")
    rows, cols = matrix.shape
    width = cols // height
    half = height // 2
    count = height * breadth
    me = r * breadth + c
    core = lax.rem(r, 2)
    chip = r // 2
    even = core == 0
    odd = core == 1
    mate = r + 1 - 2 * core
    place = 2 * (chip // 2) + lax.rem(lax.rem(chip, 2) + chip // 2, 2)

    def seat(q):
        return 2 * (2 * (q // 2) + lax.rem(q + q // 2, 2))

    root = r == 0
    edge = c == 0

    slab_copy = pltpu.make_async_copy(matrix.at[pl.ds(0, B)], slab, local_sems.at[0])
    strip_copy = pltpu.make_async_copy(matrix.at[:, pl.ds(0, 2 * B)], strip, local_sems.at[1])
    pl.when(root)(slab_copy.start)
    pl.when(edge)(strip_copy.start)
    block_copies = []
    for k in range(breadth):
        part = pl.ds(k * width, width)
        block_copies.append(pltpu.make_async_copy(matrix.at[part], block.at[part], block_sems.at[k]))
        block_copies[-1].start()

    barrier = pltpu.get_barrier_semaphore()

    def greet(step, carry):
        other = lax.rem(me + step, count)
        pl.semaphore_signal(
            barrier, inc=1, device_id=(other // breadth, lax.rem(other, breadth)), device_id_type=MESH
        )
        return carry

    lax.fori_loop(1, count, greet, 0)

    @pl.when(root)
    def _():
        slab_copy.wait()
        lane = lax.broadcasted_iota(jnp.int32, (B, cols), 1) + c * cols
        panel = jnp.where(lane >= B, slab[...], f32(0.0))
        for i in range(height):
            pc[i] = panel[:, i * width : (i + 1) * width]
        top = jnp.where(edge, slab[:, B : 2 * B], f32(0.0))
        own[...] = jnp.concatenate([product_nt(panel, panel), top], axis=1)

    pl.semaphore_wait(barrier, count - 1)

    def ring_copy(i, target):
        return remote(pc.at[i], pc.at[i], ring_sends.at[i], pc_recvs.at[i], (target, c))

    def mate_copy(i):
        return remote(pc.at[i], pc.at[i], mate_sends.at[i], pc_recvs.at[i], (mate, c))

    def part_copy(k):
        return remote(own, parts.at[c], part_sends.at[k], part_recvs.at[c], (1, k))

    forth = seat(lax.rem(place + 1, half))
    back = seat(lax.rem(place + half - 1, half))
    goes_forth = place + 1 < half
    goes_back = place != 1

    def ring_on(i):
        if i < half:
            pl.when(goes_forth)(ring_copy(i, forth).start)
        else:
            pl.when(goes_back)(ring_copy(i, back).start)

    def passed(i):
        remote(pc.at[i], pc.at[i], ring_sends.at[i], pc_recvs.at[i], (mate, c)).wait_recv()
        ring_on(i)
        mate_copy(i).start()

    @pl.when(root)
    def _():
        for k in range(breadth):
            part_copy(k).start()
        for i in range(half):
            ring_copy(i, forth).start()
            ring_copy(half + i, back).start()
        for i in range(height):
            mate_copy(i).start()

    def line_copy(k):
        return remote(pr.at[k], pr.at[k], pr_sends.at[k], pr_recvs.at[k], (r, c + 1))

    def line_received(k):
        remote(pr.at[k], pr.at[k], pr_sends.at[k], pr_recvs.at[k], (r, 0)).wait_recv()

    @pl.when(edge)
    def _():
        strip_copy.wait()
        for k in range(breadth - 1, -1, -1):
            piece = strip[k * width : (k + 1) * width, :].T[:B, :]
            lane = lax.broadcasted_iota(jnp.int32, (B, width), 1) + r * rows + k * width
            pr[k] = jnp.where(lane >= B, piece, f32(0.0))
            line_copy(k).start()

    middle = jnp.logical_and(c >= 1, c < breadth - 1)

    def line_pass(point):
        index = point - 2 * (c - 1)
        k = breadth - 1 - index

        @pl.when(jnp.logical_and(middle, jnp.logical_and(index >= 0, index < breadth)))
        def _():
            line_received(k)
            line_copy(k).start()

    relays = jnp.logical_and(even, jnp.logical_not(root))

    @pl.when(jnp.logical_and(relays, 2 * place < half))
    def _():
        for i in range(height):
            passed(i)

    @pl.when(jnp.logical_and(relays, 2 * place == half))
    def _():
        for i in range(half):
            passed(i)
            passed(half + i)

    @pl.when(jnp.logical_and(relays, 2 * place > half))
    def _():
        for i in range(height):
            passed((half + i) % height)

    def stat_copy(q):
        return remote(stats, stats, stat_sends.at[q], stat_recv, (2 * q + 1, c))

    chain_copy = remote(chained, chained, chain_send, chain_recv, (mate, c))

    @pl.when(r == 1)
    def _():
        total = None
        for k in range(breadth):
            remote(parts.at[k], parts.at[k], part_sends.at[k], part_recvs.at[k], (0, c)).wait_recv()
            total = parts[k] if total is None else total + parts[k]
        stats[...] = total
        for q in range(1, half):
            stat_copy(q).start()

    @pl.when(jnp.logical_and(odd, r != 1))
    def _():
        remote(stats, stats, stat_sends.at[0], stat_recv, (1, c)).wait_recv()

    @pl.when(odd)
    def _():
        factor, turned = factor_values(stats[:, :B], stats[:, B:].T)
        chained[...] = jnp.concatenate([factor, turned], axis=1)
        chain_copy.start()
        for i in range(height):
            remote(pc.at[i], pc.at[i], mate_sends.at[i], pc_recvs.at[i], (mate, c)).wait_recv()

    @pl.when(even)
    def _():
        for i in range(height):
            mate_copy(i).wait_send()
        chain_copy.wait_recv()

    @pl.when(root)
    def _():
        for i in range(half):
            ring_copy(i, forth).wait_send()
            ring_copy(half + i, back).wait_send()

    @pl.when(relays)
    def _():
        for i in range(half):
            pl.when(goes_forth)(ring_copy(i, forth).wait_send)
            pl.when(goes_back)(ring_copy(half + i, back).wait_send)

    def lower_top(buffer):
        for i in range(buffer.shape[0]):
            low, high = max(B, i * width), min(2 * B, (i + 1) * width)
            if low < high:
                lanes = slice(low - i * width, high - i * width)
                buffer[i, :, lanes] = buffer[i, :, lanes] - chained[:, low : high]

    @pl.when(edge)
    def _():
        lower_top(pc)

    for i in range(height):
        part = slice(i * width, (i + 1) * width)
        upper, lower = split(pc[i])
        halves[:B, part] = upper
        halves[B:, part] = lower
    for copy in block_copies:
        copy.wait()

    size = min(512, cols)

    def rs_copy(step, other):
        return remote(zs.at[other], rs.at[c], rs_sends.at[step], rs_recvs.at[c], (r, other))

    order = sorted(range(1, breadth), key=lambda s: -min(s, breadth - s)) + [0]
    for index, step in enumerate(order):
        line_pass(index)
        other = lax.rem(c + step, breadth)
        some = pl.ds(pl.multiple_of(other * width, width), width)
        both = jnp.zeros((width, 2 * B), f32)
        for start in range(0, cols, size):
            part = slice(start, start + size)
            upper, lower = split(block[some, part])
            both = both + lax.dot_general(upper, halves[:, part], NT, preferred_element_type=f32)
            low = lax.dot_general(lower, halves[:, part], NT, preferred_element_type=f32)
            both = both + jnp.where(lax.broadcasted_iota(jnp.int32, both.shape, 1) < B, low, f32(0.0))
        turned = both.T
        value = turned[:B, :] + turned[B:, :]
        if step:
            zs[other] = value
            rs_copy(step, other).start()
        else:
            rs[c] = value
    for index in range(breadth, breadth + 2 * max(0, breadth - 3)):
        line_pass(index)

    for step in range(1, breadth):
        other = lax.rem(c + step, breadth)
        remote(rs.at[other], rs.at[other], rs_sends.at[step], rs_recvs.at[other], (r, other)).wait_recv()
    total = rs[0]
    for k in range(1, breadth):
        total = total + rs[k]
    wr[c] = total

    def right_copy(k):
        return remote(wr.at[k], wr.at[k], wr_right.at[k], wr_recvs.at[k], (r, c + 1))

    def left_copy(k):
        return remote(wr.at[k], wr.at[k], wr_left.at[k], wr_recvs.at[k], (r, c - 1))

    has_right = c + 1 < breadth
    has_left = c >= 1
    to_row = lax.rem(me, height)
    to_col = me // height
    itself = jnp.logical_and(to_row == r, to_col == c)
    role = remote(wr.at[c], wc.at[to_row], role_send, wc_recvs.at[to_row], (to_row, to_col))
    pl.when(has_right)(right_copy(c).start)
    pl.when(has_left)(left_copy(c).start)
    pl.when(jnp.logical_not(itself))(role.start)

    @pl.when(itself)
    def _():
        wc[r] = total

    @pl.when(c == breadth - 1)
    def _():
        line_received(breadth - 1)

    slots = lax.broadcasted_iota(jnp.int32, (B, width), 0)
    positions = lax.broadcasted_iota(jnp.int32, (B, width), 1) + me * width - B
    onehot = jnp.where(positions == slots, f32(1.0), f32(0.0))
    vector = pr[c] - product(chained[:, B:], onehot)
    pe[r] = jnp.concatenate([product_nt(total, vector), jnp.zeros((B, B), f32)], axis=1)

    def pe_copy(step):
        other = lax.rem(r + step, height)
        return remote(pe.at[r], pe.at[r], pe_sends.at[step], pe_recvs.at[r], (other, c)), other

    for step in range(1, height):
        pe_copy(step)[0].start()

    def wr_pass(s):
        @pl.when(c - s >= 0)
        def _():
            remote(wr.at[c - s], wr.at[c - s], wr_right.at[0], wr_recvs.at[c - s], (r, c - 1)).wait_recv()
            pl.when(has_right)(right_copy(c - s).start)

        @pl.when(c + s < breadth)
        def _():
            remote(wr.at[c + s], wr.at[c + s], wr_left.at[0], wr_recvs.at[c + s], (r, c + 1)).wait_recv()
            pl.when(has_left)(left_copy(c + s).start)

    def wc_copy(slot, step, other):
        return remote(wc.at[slot], wc.at[slot], wc_sends.at[step], wc_recvs.at[slot], (other, c))

    def wc_received(slot):
        remote(wc.at[slot], wc.at[slot], wc_sends.at[0], wc_recvs.at[slot], (mate, c)).wait_recv()

    pl.when(jnp.logical_not(itself))(lambda: wc_received(r))
    for step in range(2, height, 2):
        wc_copy(r, step, lax.rem(r + step, height)).start()
    wc_copy(r, 1, mate).start()
    wr_pass(1)
    summed = pe[r]
    for step in range(1, height):
        copy, other = pe_copy(step)
        remote(pe.at[other], pe.at[other], pe_sends.at[step], pe_recvs.at[other], (other, c)).wait_recv()
        summed = summed + pe[other]
    ps[c] = summed

    def ps_copy(step):
        other = lax.rem(c + step, breadth)
        return remote(ps.at[c], ps.at[c], pt_sends.at[step], pt_recvs.at[c], (r, other)), other

    for step in range(1, breadth):
        ps_copy(step)[0].start()
    for step in range(2, height, 2):
        slot = lax.rem(r + step, height)
        wc_received(slot)
        wc_copy(slot, step + 1, mate).start()
    for s in range(2, breadth):
        wr_pass(s)
    projected = ps[c]
    for step in range(1, breadth):
        copy, other = ps_copy(step)
        remote(ps.at[other], ps.at[other], pt_sends.at[step], pt_recvs.at[other], (r, other)).wait_recv()
        projected = projected + ps[other]

    factor = chained[:, :B]
    turned = factor.T
    inner = product(turned, product(projected[:, :B], factor))
    mix = jnp.concatenate([turned, -0.5 * inner], axis=1)
    wc_received(mate)
    for step in range(2, height, 2):
        wc_received(lax.rem(mate + step, height))
    for i in range(height):
        part = slice(i * width, (i + 1) * width)
        v = pc[i]
        u = product(mix, jnp.concatenate([wc[i], v], axis=0))
        upper, lower = split(jnp.concatenate([u, v], axis=0))
        right[: 2 * B, part] = upper
        right[2 * B : 4 * B, part] = upper
        right[4 * B :, part] = lower

    @pl.when(c == breadth - 1)
    def _():
        for k in range(breadth - 1):
            line_received(k)

    @pl.when(c < breadth - 1)
    def _():
        for k in range(breadth):
            line_copy(k).wait_send()

    @pl.when(root)
    def _():
        lower_top(pr)

    for i in range(breadth):
        part = slice(i * width, (i + 1) * width)
        v = pr[i]
        u = product(mix, jnp.concatenate([wr[i], v], axis=0))
        upper, lower = split(jnp.concatenate([v, u], axis=0).T)
        left[part, : 2 * B] = upper
        left[part, 2 * B : 4 * B] = lower
        left[part, 4 * B :] = upper

    @pl.when(root)
    def _():
        for k in range(breadth):
            part_copy(k).wait_send()

    @pl.when(r == 1)
    def _():
        for q in range(1, half):
            stat_copy(q).wait_send()

    pl.when(odd)(chain_copy.wait_send)
    for step in range(1, breadth):
        rs_copy(step, lax.rem(c + step, breadth)).wait_send()
        ps_copy(step)[0].wait_send()
    for step in range(1, height):
        pe_copy(step)[0].wait_send()
    pl.when(jnp.logical_not(itself))(role.wait_send)
    for step in range(2, height, 2):
        wc_copy(r, step, lax.rem(r + step, height)).wait_send()
        wc_copy(lax.rem(r + step, height), step + 1, mate).wait_send()
    wc_copy(r, 1, mate).wait_send()

    @pl.when(has_right)
    def _():
        for k in range(breadth):
            pl.when(k <= c)(right_copy(k).wait_send)

    @pl.when(has_left)
    def _():
        for k in range(breadth):
            pl.when(k >= c)(left_copy(k).wait_send)


def front(matrix, height, breadth):
    rows, cols = matrix.shape
    width = cols // height
    vmem = pl.BlockSpec(memory_space=pltpu.VMEM)
    dma = pltpu.SemaphoreType.DMA
    scratch = [
        pltpu.VMEM((B, cols), f32),
        pltpu.VMEM((rows, 2 * B), f32),
        pltpu.VMEM((height, B, width), f32),
        pltpu.VMEM((breadth, B, width), f32),
        pltpu.VMEM((2 * B, cols), bf16),
        pltpu.VMEM((B, 2 * B), f32),
        pltpu.VMEM((breadth, B, 2 * B), f32),
        pltpu.VMEM((B, 2 * B), f32),
        pltpu.VMEM((B, 2 * B), f32),
        pltpu.VMEM((breadth, B, width), f32),
        pltpu.VMEM((breadth, B, width), f32),
        pltpu.VMEM((breadth, B, width), f32),
        pltpu.VMEM((height, B, width), f32),
        pltpu.VMEM((height, B, 2 * B), f32),
        pltpu.VMEM((breadth, B, 2 * B), f32),
        pltpu.VMEM((B, 2 * B), f32),
        dma((2,)),
        dma((breadth,)),
        dma((height,)),
        dma((height,)),
        dma((height,)),
        dma((breadth,)),
        dma((breadth,)),
        dma((breadth,)),
        dma((breadth,)),
        dma((height // 2,)),
        dma(()),
        dma(()),
        dma(()),
        dma((breadth,)),
        dma((breadth,)),
        dma((breadth,)),
        dma((breadth,)),
        dma((breadth,)),
        dma(()),
        dma((height,)),
        dma((height,)),
        dma((height,)),
        dma((height,)),
        dma((breadth,)),
        dma((breadth,)),
    ]
    return pl.pallas_call(
        lambda *refs: front_kernel(height, breadth, *refs),
        out_shape=[
            pltpu.VMEM((rows, cols), f32),
            pltpu.VMEM((rows, 6 * B), bf16),
            pltpu.VMEM((6 * B, cols), bf16),
        ],
        in_specs=[pl.BlockSpec(memory_space=pl.ANY)],
        out_specs=[vmem] * 3,
        scratch_shapes=scratch,
        compiler_params=pltpu.CompilerParams(
            collective_id=0, has_side_effects=True, vmem_limit_bytes=20 << 20
        ),
        name="front",
    )(matrix)


def final_kernel(tile, slots, block, left, right, out, buffer, sems):
    rows, cols = block.shape
    size = min(512, cols)
    count = rows // tile

    def copy(i):
        return pltpu.make_async_copy(
            buffer.at[i % slots], out.at[pl.ds(i * tile, tile)], sems.at[i % slots]
        )

    for i in range(count):
        if i >= slots:
            copy(i - slots).wait()
        some = slice(i * tile, (i + 1) * tile)
        for start in range(0, cols, size):
            part = slice(start, start + size)
            buffer[i % slots, :, part] = block[some, part] - jnp.dot(
                left[some, :], right[:, part], preferred_element_type=f32
            )
        copy(i).start()
    for i in range(max(0, count - slots), count):
        copy(i).wait()


def final(block, left, right):
    rows, cols = block.shape
    tile = min(256, rows)
    slots = min(4, rows // tile)
    vmem = pl.BlockSpec(memory_space=pltpu.VMEM)
    held = [pltpu.with_memory_space_constraint(x, pltpu.VMEM) for x in (block, left, right)]
    return pl.pallas_call(
        lambda *refs: final_kernel(tile, slots, *refs),
        out_shape=jax.ShapeDtypeStruct((rows, cols), f32),
        in_specs=[vmem] * 3,
        out_specs=pl.BlockSpec(memory_space=pl.ANY),
        scratch_shapes=[
            pltpu.VMEM((slots, tile, cols), f32),
            pltpu.SemaphoreType.DMA((slots,)),
        ],
        compiler_params=pltpu.CompilerParams(vmem_limit_bytes=20 << 20),
        name="final",
    )(*held)


def solution(mesh):
    height, breadth = mesh.shape["row"], mesh.shape["col"]

    def shards(matrix):
        return final(*front(matrix, height, breadth))

    return jax.shard_map(
        shards,
        mesh=mesh,
        in_specs=(P("row", "col"),),
        out_specs=P("row", "col"),
        check_vma=False,
    )
```

```python
import jax
import jax.numpy as jnp
from jax import lax
from jax.experimental import pallas as pl
from jax.experimental.pallas import tpu as pltpu
from jax.sharding import PartitionSpec as P

B = 64
STEP = 8


highest = lax.Precision.HIGHEST
MESH = pl.DeviceIdType.MESH
f32 = jnp.float32
bf16 = jnp.bfloat16
NT = (((1,), (1,)), ((), ()))
TN = (((0,), (0,)), ((), ()))


def product(left, right):
    return jnp.dot(left, right, precision=highest, preferred_element_type=f32)


def product_nt(left, right):
    return lax.dot_general(left, right, NT, precision=highest, preferred_element_type=f32)


def product_tn(left, right):
    return lax.dot_general(left, right, TN, precision=highest, preferred_element_type=f32)


def split(x):
    upper = x.astype(bf16)
    return upper, (x - upper.astype(f32)).astype(bf16)


def eliminate(work, rows):
    for j in range(0, B, STEP):
        columns = [jnp.broadcast_to(work[:, j + k : j + k + 1], work.shape) for k in range(STEP)]
        lines = [work[j + k : j + k + 1, :] for k in range(STEP)]
        small = [[columns[c][j + r : j + r + 1, :] for c in range(STEP)] for r in range(STEP)]
        scaled = []
        for k in range(STEP):
            inverse = 1.0 / small[k][k]
            scaled.append(lines[k] * inverse)
            for m in range(k + 1, STEP):
                ratio = small[k][m] * inverse
                columns[m] = columns[m] - columns[k] * ratio
                lines[m] = lines[m] - lines[k] * ratio
                for c in range(m, STEP):
                    small[m][c] = small[m][c] - ratio * small[k][c]
        lowered = work
        for k in range(STEP):
            lowered = lowered - columns[k] * scaled[k]
        lowered = jnp.where(rows >= j + STEP, lowered, work)
        for k in range(1, STEP):
            lowered = jnp.where(rows == j + k, lines[k], lowered)
        work = lowered
    return work


def sign_inverse(q, rows):
    lane = lax.broadcasted_iota(jnp.int32, (1, 2 * B), 1)
    signs = jnp.zeros((B, 2 * B), f32)
    for j in range(0, B, STEP):
        columns = [jnp.broadcast_to(q[:, j + k : j + k + 1], q.shape) for k in range(STEP)]
        lines = [q[j + k : j + k + 1, :] for k in range(STEP)]
        small = [[columns[c][j + r : j + r + 1, :] for c in range(STEP)] for r in range(STEP)]
        scaled = []
        chosen = []
        for k in range(STEP):
            sign = jnp.where(small[k][k] >= 0, f32(-1.0), f32(1.0))
            pivot = small[k][k] - sign
            inverse = 1.0 / pivot
            chosen.append(sign)
            lines[k] = jnp.where(lane == j + k, pivot, lines[k]) * inverse
            scaled.append(lines[k])
            for c in range(k + 1, STEP):
                small[k][c] = small[k][c] * inverse
                columns[c] = columns[c] - columns[k] * small[k][c]
            for r in range(STEP):
                if r != k:
                    lines[r] = lines[r] - small[r][k] * lines[k]
                    for c in range(k + 1, STEP):
                        small[r][c] = small[r][c] - small[r][k] * small[k][c]
        for k in range(STEP):
            q = q - columns[k] * scaled[k]
        for k in range(STEP):
            q = jnp.where(rows == j + k, lines[k], q)
            signs = jnp.where(rows == j + k, chosen[k], signs)
    return q[:, B:], signs[:, :1]


def factor_values(gram, top):
    rows = lax.broadcasted_iota(jnp.int32, (B, 2 * B), 0)
    lanes = lax.broadcasted_iota(jnp.int32, (B, 2 * B), 1)
    small_rows = lax.broadcasted_iota(jnp.int32, (B, B), 0)
    small_lanes = lax.broadcasted_iota(jnp.int32, (B, B), 1)
    eye = jnp.where(small_rows == small_lanes, f32(1.0), f32(0.0))
    work = eliminate(jnp.concatenate([gram, eye], axis=1), rows)
    pivots = jnp.sum(jnp.where(rows == lanes, work, f32(0.0)), axis=1, keepdims=True)
    work = work * (1.0 / jnp.sqrt(pivots))
    upper = jnp.where(small_lanes >= small_rows, work[:, :B], f32(0.0))
    lower_inverse = work[:, B:]
    basis = product_nt(top, lower_inverse)
    inverse, signs = sign_inverse(jnp.concatenate([basis, eye], axis=1), rows)
    factor = -product_tn(lower_inverse, product(signs * inverse.T, lower_inverse))
    return factor, (signs * upper).T


def remote(src, dst, send_sem, recv_sem, device):
    return pltpu.make_async_remote_copy(
        src_ref=src,
        dst_ref=dst,
        send_sem=send_sem,
        recv_sem=recv_sem,
        device_id=device,
        device_id_type=MESH,
    )


def front_kernel(
    height, breadth, matrix, block, left, right,
    slab, strip, pc, pr, halves, own, parts, stats, chained, zs, rs, wr, wc, pe, ps, pt,
    local_sems, block_sems, pc_recvs, ring_sends, mate_sends, pr_recvs, pr_sends, part_sends, part_recvs,
    stat_sends, stat_recv, chain_send, chain_recv, rs_sends, rs_recvs, wr_right, wr_left, wr_recvs,
    role_send, wc_recvs, wc_sends, pe_sends, pe_recvs, pt_sends, pt_recvs,
):
    r, c = lax.axis_index("row"), lax.axis_index("col")
    rows, cols = matrix.shape
    width = cols // height
    half = height // 2
    count = height * breadth
    me = r * breadth + c
    core = lax.rem(r, 2)
    chip = r // 2
    even = core == 0
    odd = core == 1
    mate = r + 1 - 2 * core
    place = 2 * (chip // 2) + lax.rem(lax.rem(chip, 2) + chip // 2, 2)

    def seat(q):
        return 2 * (2 * (q // 2) + lax.rem(q + q // 2, 2))

    root = r == 0
    edge = c == 0

    slab_copy = pltpu.make_async_copy(matrix.at[pl.ds(0, B)], slab, local_sems.at[0])
    strip_copy = pltpu.make_async_copy(matrix.at[:, pl.ds(0, 2 * B)], strip, local_sems.at[1])
    pl.when(root)(slab_copy.start)
    pl.when(edge)(strip_copy.start)
    block_copies = []
    for k in range(breadth):
        part = pl.ds(k * width, width)
        block_copies.append(pltpu.make_async_copy(matrix.at[part], block.at[part], block_sems.at[k]))

    barrier = pltpu.get_barrier_semaphore()

    def greet(step, carry):
        other = lax.rem(me + step, count)
        pl.semaphore_signal(
            barrier, inc=1, device_id=(other // breadth, lax.rem(other, breadth)), device_id_type=MESH
        )
        return carry

    lax.fori_loop(1, count, greet, 0)

    def masked_slab():
        lane = lax.broadcasted_iota(jnp.int32, (B, cols), 1) + c * cols
        return jnp.where(lane >= B, slab[...], f32(0.0))

    @pl.when(root)
    def _():
        slab_copy.wait()
        panel = masked_slab()
        for i in range(height):
            pc[i] = panel[:, i * width : (i + 1) * width]

    pl.when(edge)(strip_copy.wait)
    for copy in block_copies:
        copy.start()

    @pl.when(root)
    def _():
        panel = masked_slab()
        top = jnp.where(edge, slab[:, B : 2 * B], f32(0.0))
        own[...] = jnp.concatenate([product_nt(panel, panel), top], axis=1)

    @pl.when(edge)
    def _():
        for k in range(breadth):
            piece = strip[k * width : (k + 1) * width, :].T[:B, :]
            lane = lax.broadcasted_iota(jnp.int32, (B, width), 1) + r * rows + k * width
            pr[k] = jnp.where(lane >= B, piece, f32(0.0))

    pl.semaphore_wait(barrier, count - 1)

    def piece_copy(i, part, sends, target):
        some = pc.at[i, pl.ds(part * (B // 2), B // 2)]
        return remote(some, some, sends.at[i, part], pc_recvs.at[i, part], (target, c))

    def ring_copy(i, part, target):
        return piece_copy(i, part, ring_sends, target)

    def mate_copy(i, part):
        return piece_copy(i, part, mate_sends, mate)

    def part_copy(k):
        return remote(own, parts.at[c], part_sends.at[k], part_recvs.at[c], (1, k))

    forth = seat(lax.rem(place + 1, half))
    back = seat(lax.rem(place + half - 1, half))
    goes_forth = place + 1 < half
    goes_back = place != 1

    def ring_on(i, part):
        if i < half:
            pl.when(goes_forth)(ring_copy(i, part, forth).start)
        else:
            pl.when(goes_back)(ring_copy(i, part, back).start)

    def passed(i, part):
        mate_copy(i, part).wait_recv()
        ring_on(i, part)
        mate_copy(i, part).start()

    @pl.when(root)
    def _():
        for k in range(breadth):
            part_copy(k).start()
        for i in range(half):
            for part in range(2):
                ring_copy(i, part, forth).start()
                ring_copy(half + i, part, back).start()
        for i in range(height):
            for part in range(2):
                mate_copy(i, part).start()

    def line_copy(k):
        return remote(pr.at[k], pr.at[k], pr_sends.at[k], pr_recvs.at[k], (r, c + 1))

    def line_received(k):
        remote(pr.at[k], pr.at[k], pr_sends.at[k], pr_recvs.at[k], (r, 0)).wait_recv()

    @pl.when(edge)
    def _():
        for k in range(breadth - 1, -1, -1):
            line_copy(k).start()

    middle = jnp.logical_and(c >= 1, c < breadth - 1)

    def line_pass(who, index):
        k = breadth - 1 - index

        @pl.when(jnp.logical_and(middle, c == who))
        def _():
            line_received(k)
            line_copy(k).start()

    relays = jnp.logical_and(even, jnp.logical_not(root))

    def go_round(pieces):
        for step, (i, part) in enumerate(pieces):
            passed(i, part)
            for index in range(breadth):
                if (index + 1) * len(pieces) // breadth - 1 == step:
                    line_pass(1, index)

    pieces = [(i, part) for i in range(height) for part in range(2)]
    later = pieces[height:] + pieces[:height]

    @pl.when(jnp.logical_and(relays, 2 * place < half))
    def _():
        go_round(pieces)

    @pl.when(jnp.logical_and(relays, 2 * place == half))
    def _():
        go_round([piece for pair in zip(pieces[:height], later[:height]) for piece in pair])

    @pl.when(jnp.logical_and(relays, 2 * place > half))
    def _():
        go_round(later)

    @pl.when(root)
    def _():
        for index in range(breadth):
            line_pass(1, index)

    def stat_copy(q):
        return remote(stats, stats, stat_sends.at[q], stat_recv, (2 * q + 1, c))

    chain_copy = remote(chained, chained, chain_send, chain_recv, (mate, c))

    @pl.when(r == 1)
    def _():
        total = None
        for k in range(breadth):
            remote(parts.at[k], parts.at[k], part_sends.at[k], part_recvs.at[k], (0, c)).wait_recv()
            total = parts[k] if total is None else total + parts[k]
        stats[...] = total
        for q in range(1, half):
            stat_copy(q).start()

    pl.when(odd)(lambda: line_pass(1, 0))

    @pl.when(jnp.logical_and(odd, r != 1))
    def _():
        remote(stats, stats, stat_sends.at[0], stat_recv, (1, c)).wait_recv()

    @pl.when(odd)
    def _():
        factor, turned = factor_values(stats[:, :B], stats[:, B:].T)
        chained[...] = jnp.concatenate([factor, turned], axis=1)
        chain_copy.start()
        for index in range(1, breadth):
            line_pass(1, index)
        for i, part in pieces:
            mate_copy(i, part).wait_recv()

    @pl.when(even)
    def _():
        for i, part in pieces:
            mate_copy(i, part).wait_send()
        chain_copy.wait_recv()

    @pl.when(root)
    def _():
        for i, part in pieces[:height]:
            ring_copy(i, part, forth).wait_send()
            ring_copy(half + i, part, back).wait_send()

    @pl.when(relays)
    def _():
        for i, part in pieces[:height]:
            pl.when(goes_forth)(ring_copy(i, part, forth).wait_send)
            pl.when(goes_back)(ring_copy(half + i, part, back).wait_send)

    def lower_top(buffer):
        for i in range(buffer.shape[0]):
            low, high = max(B, i * width), min(2 * B, (i + 1) * width)
            if low < high:
                lanes = slice(low - i * width, high - i * width)
                buffer[i, :, lanes] = buffer[i, :, lanes] - chained[:, low : high]

    @pl.when(edge)
    def _():
        lower_top(pc)

    for i in range(height):
        part = slice(i * width, (i + 1) * width)
        upper, lower = split(pc[i])
        halves[:B, part] = upper
        halves[B:, part] = lower
    for copy in block_copies:
        copy.wait()

    size = min(512, cols)

    def rs_copy(step, other):
        return remote(zs.at[other], rs.at[c], rs_sends.at[step], rs_recvs.at[c], (r, other))

    order = sorted(range(1, breadth), key=lambda s: -min(s, breadth - s)) + [0]
    for index, step in enumerate(order):
        if index < 3:
            bounds = [0, breadth // 2, 3 * breadth // 4, breadth]
            for k in range(bounds[index], bounds[index + 1]):
                line_pass(2, k)
        other = lax.rem(c + step, breadth)
        some = pl.ds(pl.multiple_of(other * width, width), width)
        both = jnp.zeros((width, 2 * B), f32)
        for start in range(0, cols, size):
            part = slice(start, start + size)
            upper, lower = split(block[some, part])
            both = both + lax.dot_general(upper, halves[:, part], NT, preferred_element_type=f32)
            low = lax.dot_general(lower, halves[:, part], NT, preferred_element_type=f32)
            both = both + jnp.where(lax.broadcasted_iota(jnp.int32, both.shape, 1) < B, low, f32(0.0))
        turned = both.T
        value = turned[:B, :] + turned[B:, :]
        if step:
            zs[other] = value
            rs_copy(step, other).start()
        else:
            rs[c] = value
    for who in range(3, breadth - 1):
        for k in range(breadth):
            line_pass(who, k)

    for step in range(1, breadth):
        other = lax.rem(c + step, breadth)
        remote(rs.at[other], rs.at[other], rs_sends.at[step], rs_recvs.at[other], (r, other)).wait_recv()
    total = rs[0]
    for k in range(1, breadth):
        total = total + rs[k]
    wr[c] = total

    def right_copy(k):
        return remote(wr.at[k], wr.at[k], wr_right.at[k], wr_recvs.at[k], (r, c + 1))

    def left_copy(k):
        return remote(wr.at[k], wr.at[k], wr_left.at[k], wr_recvs.at[k], (r, c - 1))

    has_right = c + 1 < breadth
    has_left = c >= 1
    to_row = lax.rem(me, height)
    to_col = me // height
    itself = jnp.logical_and(to_row == r, to_col == c)
    role = remote(wr.at[c], wc.at[to_row], role_send, wc_recvs.at[to_row], (to_row, to_col))
    pl.when(has_right)(right_copy(c).start)
    pl.when(has_left)(left_copy(c).start)
    pl.when(jnp.logical_not(itself))(role.start)

    @pl.when(itself)
    def _():
        wc[r] = total

    @pl.when(c == breadth - 1)
    def _():
        line_received(breadth - 1)

    slots = lax.broadcasted_iota(jnp.int32, (B, width), 0)
    positions = lax.broadcasted_iota(jnp.int32, (B, width), 1) + me * width - B
    onehot = jnp.where(positions == slots, f32(1.0), f32(0.0))
    vector = pr[c] - product(chained[:, B:], onehot)
    pe[r] = jnp.concatenate([product_nt(total, vector), jnp.zeros((B, B), f32)], axis=1)

    def pe_copy(step):
        other = lax.rem(r + step, height)
        return remote(pe.at[r], pe.at[r], pe_sends.at[step], pe_recvs.at[r], (other, c)), other

    for step in range(1, height):
        pe_copy(step)[0].start()

    def wr_pass(s):
        @pl.when(c - s >= 0)
        def _():
            remote(wr.at[c - s], wr.at[c - s], wr_right.at[0], wr_recvs.at[c - s], (r, c - 1)).wait_recv()
            pl.when(has_right)(right_copy(c - s).start)

        @pl.when(c + s < breadth)
        def _():
            remote(wr.at[c + s], wr.at[c + s], wr_left.at[0], wr_recvs.at[c + s], (r, c + 1)).wait_recv()
            pl.when(has_left)(left_copy(c + s).start)

    def wc_copy(slot, step, other):
        return remote(wc.at[slot], wc.at[slot], wc_sends.at[step], wc_recvs.at[slot], (other, c))

    def wc_received(slot):
        remote(wc.at[slot], wc.at[slot], wc_sends.at[0], wc_recvs.at[slot], (mate, c)).wait_recv()

    pl.when(jnp.logical_not(itself))(lambda: wc_received(r))
    for step in range(2, height, 2):
        wc_copy(r, step, lax.rem(r + step, height)).start()
    wc_copy(r, 1, mate).start()
    wr_pass(1)
    summed = pe[r]
    for step in range(1, height):
        copy, other = pe_copy(step)
        remote(pe.at[other], pe.at[other], pe_sends.at[step], pe_recvs.at[other], (other, c)).wait_recv()
        summed = summed + pe[other]
    ps[c] = summed

    def ps_copy(step):
        other = lax.rem(c + step, breadth)
        return remote(ps.at[c], ps.at[c], pt_sends.at[step], pt_recvs.at[c], (r, other)), other

    for step in range(1, breadth):
        ps_copy(step)[0].start()
    for step in range(2, height, 2):
        slot = lax.rem(r + step, height)
        wc_received(slot)
        wc_copy(slot, step + 1, mate).start()
    for s in range(2, breadth):
        wr_pass(s)
    projected = ps[c]
    for step in range(1, breadth):
        copy, other = ps_copy(step)
        remote(ps.at[other], ps.at[other], pt_sends.at[step], pt_recvs.at[other], (r, other)).wait_recv()
        projected = projected + ps[other]

    factor = chained[:, :B]
    turned = factor.T
    inner = product(turned, product(projected[:, :B], factor))
    mix = jnp.concatenate([turned, -0.5 * inner], axis=1)
    wc_received(mate)
    for step in range(2, height, 2):
        wc_received(lax.rem(mate + step, height))
    for i in range(height):
        part = slice(i * width, (i + 1) * width)
        v = pc[i]
        u = product(mix, jnp.concatenate([wc[i], v], axis=0))
        upper, lower = split(jnp.concatenate([u, v], axis=0))
        right[: 2 * B, part] = upper
        right[2 * B : 4 * B, part] = upper
        right[4 * B :, part] = lower

    @pl.when(c == breadth - 1)
    def _():
        for k in range(breadth - 1):
            line_received(k)

    @pl.when(c < breadth - 1)
    def _():
        for k in range(breadth):
            line_copy(k).wait_send()

    @pl.when(root)
    def _():
        lower_top(pr)

    for i in range(breadth):
        part = slice(i * width, (i + 1) * width)
        v = pr[i]
        u = product(mix, jnp.concatenate([wr[i], v], axis=0))
        upper, lower = split(jnp.concatenate([v, u], axis=0).T)
        left[part, : 2 * B] = upper
        left[part, 2 * B : 4 * B] = lower
        left[part, 4 * B :] = upper

    @pl.when(root)
    def _():
        for k in range(breadth):
            part_copy(k).wait_send()

    @pl.when(r == 1)
    def _():
        for q in range(1, half):
            stat_copy(q).wait_send()

    pl.when(odd)(chain_copy.wait_send)
    for step in range(1, breadth):
        rs_copy(step, lax.rem(c + step, breadth)).wait_send()
        ps_copy(step)[0].wait_send()
    for step in range(1, height):
        pe_copy(step)[0].wait_send()
    pl.when(jnp.logical_not(itself))(role.wait_send)
    for step in range(2, height, 2):
        wc_copy(r, step, lax.rem(r + step, height)).wait_send()
        wc_copy(lax.rem(r + step, height), step + 1, mate).wait_send()
    wc_copy(r, 1, mate).wait_send()

    @pl.when(has_right)
    def _():
        for k in range(breadth):
            pl.when(k <= c)(right_copy(k).wait_send)

    @pl.when(has_left)
    def _():
        for k in range(breadth):
            pl.when(k >= c)(left_copy(k).wait_send)


def front(matrix, height, breadth):
    rows, cols = matrix.shape
    width = cols // height
    vmem = pl.BlockSpec(memory_space=pltpu.VMEM)
    dma = pltpu.SemaphoreType.DMA
    scratch = [
        pltpu.VMEM((B, cols), f32),
        pltpu.VMEM((rows, 2 * B), f32),
        pltpu.VMEM((height, B, width), f32),
        pltpu.VMEM((breadth, B, width), f32),
        pltpu.VMEM((2 * B, cols), bf16),
        pltpu.VMEM((B, 2 * B), f32),
        pltpu.VMEM((breadth, B, 2 * B), f32),
        pltpu.VMEM((B, 2 * B), f32),
        pltpu.VMEM((B, 2 * B), f32),
        pltpu.VMEM((breadth, B, width), f32),
        pltpu.VMEM((breadth, B, width), f32),
        pltpu.VMEM((breadth, B, width), f32),
        pltpu.VMEM((height, B, width), f32),
        pltpu.VMEM((height, B, 2 * B), f32),
        pltpu.VMEM((breadth, B, 2 * B), f32),
        pltpu.VMEM((B, 2 * B), f32),
        dma((2,)),
        dma((breadth,)),
        dma((height, 2)),
        dma((height, 2)),
        dma((height, 2)),
        dma((breadth,)),
        dma((breadth,)),
        dma((breadth,)),
        dma((breadth,)),
        dma((height // 2,)),
        dma(()),
        dma(()),
        dma(()),
        dma((breadth,)),
        dma((breadth,)),
        dma((breadth,)),
        dma((breadth,)),
        dma((breadth,)),
        dma(()),
        dma((height,)),
        dma((height,)),
        dma((height,)),
        dma((height,)),
        dma((breadth,)),
        dma((breadth,)),
    ]
    return pl.pallas_call(
        lambda *refs: front_kernel(height, breadth, *refs),
        out_shape=[
            pltpu.VMEM((rows, cols), f32),
            pltpu.VMEM((rows, 6 * B), bf16),
            pltpu.VMEM((6 * B, cols), bf16),
        ],
        in_specs=[pl.BlockSpec(memory_space=pl.ANY)],
        out_specs=[vmem] * 3,
        scratch_shapes=scratch,
        compiler_params=pltpu.CompilerParams(
            collective_id=0, has_side_effects=True, vmem_limit_bytes=20 << 20
        ),
        name="front",
    )(matrix)


def final_kernel(tile, slots, block, left, right, out, buffer, sems):
    rows, cols = block.shape
    size = min(512, cols)
    count = rows // tile

    def copy(i):
        return pltpu.make_async_copy(
            buffer.at[i % slots], out.at[pl.ds(i * tile, tile)], sems.at[i % slots]
        )

    for i in range(count):
        if i >= slots:
            copy(i - slots).wait()
        some = slice(i * tile, (i + 1) * tile)
        for start in range(0, cols, size):
            part = slice(start, start + size)
            buffer[i % slots, :, part] = block[some, part] - jnp.dot(
                left[some, :], right[:, part], preferred_element_type=f32
            )
        copy(i).start()
    for i in range(max(0, count - slots), count):
        copy(i).wait()


def final(block, left, right):
    rows, cols = block.shape
    tile = min(256, rows)
    slots = min(4, rows // tile)
    vmem = pl.BlockSpec(memory_space=pltpu.VMEM)
    held = [pltpu.with_memory_space_constraint(x, pltpu.VMEM) for x in (block, left, right)]
    return pl.pallas_call(
        lambda *refs: final_kernel(tile, slots, *refs),
        out_shape=jax.ShapeDtypeStruct((rows, cols), f32),
        in_specs=[vmem] * 3,
        out_specs=pl.BlockSpec(memory_space=pl.ANY),
        scratch_shapes=[
            pltpu.VMEM((slots, tile, cols), f32),
            pltpu.SemaphoreType.DMA((slots,)),
        ],
        compiler_params=pltpu.CompilerParams(vmem_limit_bytes=20 << 20),
        name="final",
    )(*held)


def solution(mesh):
    height, breadth = mesh.shape["row"], mesh.shape["col"]

    def shards(matrix):
        return final(*front(matrix, height, breadth))

    return jax.shard_map(
        shards,
        mesh=mesh,
        in_specs=(P("row", "col"),),
        out_specs=P("row", "col"),
        check_vma=False,
    )
```

```python
import jax
import jax.numpy as jnp
from jax import lax
from jax.experimental import pallas as pl
from jax.experimental.pallas import tpu as pltpu
from jax.sharding import PartitionSpec as P

B = 64
STEP = 8


highest = lax.Precision.HIGHEST
MESH = pl.DeviceIdType.MESH
f32 = jnp.float32
bf16 = jnp.bfloat16
NT = (((1,), (1,)), ((), ()))
TN = (((0,), (0,)), ((), ()))


def product(left, right):
    return jnp.dot(left, right, precision=highest, preferred_element_type=f32)


def product_nt(left, right):
    return lax.dot_general(left, right, NT, precision=highest, preferred_element_type=f32)


def product_tn(left, right):
    return lax.dot_general(left, right, TN, precision=highest, preferred_element_type=f32)


def split(x):
    upper = x.astype(bf16)
    return upper, (x - upper.astype(f32)).astype(bf16)


def eliminate(work, rows):
    for j in range(0, B, STEP):
        columns = [jnp.broadcast_to(work[:, j + k : j + k + 1], work.shape) for k in range(STEP)]
        lines = [work[j + k : j + k + 1, :] for k in range(STEP)]
        small = [[columns[c][j + r : j + r + 1, :] for c in range(STEP)] for r in range(STEP)]
        scaled = []
        for k in range(STEP):
            inverse = 1.0 / small[k][k]
            scaled.append(lines[k] * inverse)
            for m in range(k + 1, STEP):
                ratio = small[k][m] * inverse
                columns[m] = columns[m] - columns[k] * ratio
                lines[m] = lines[m] - lines[k] * ratio
                for c in range(m, STEP):
                    small[m][c] = small[m][c] - ratio * small[k][c]
        lowered = work
        for k in range(STEP):
            lowered = lowered - columns[k] * scaled[k]
        lowered = jnp.where(rows >= j + STEP, lowered, work)
        for k in range(1, STEP):
            lowered = jnp.where(rows == j + k, lines[k], lowered)
        work = lowered
    return work


def sign_inverse(q, rows):
    lane = lax.broadcasted_iota(jnp.int32, (1, 2 * B), 1)
    signs = jnp.zeros((B, 2 * B), f32)
    for j in range(0, B, STEP):
        columns = [jnp.broadcast_to(q[:, j + k : j + k + 1], q.shape) for k in range(STEP)]
        lines = [q[j + k : j + k + 1, :] for k in range(STEP)]
        small = [[columns[c][j + r : j + r + 1, :] for c in range(STEP)] for r in range(STEP)]
        scaled = []
        chosen = []
        for k in range(STEP):
            sign = jnp.where(small[k][k] >= 0, f32(-1.0), f32(1.0))
            pivot = small[k][k] - sign
            inverse = 1.0 / pivot
            chosen.append(sign)
            lines[k] = jnp.where(lane == j + k, pivot, lines[k]) * inverse
            scaled.append(lines[k])
            for c in range(k + 1, STEP):
                small[k][c] = small[k][c] * inverse
                columns[c] = columns[c] - columns[k] * small[k][c]
            for r in range(STEP):
                if r != k:
                    lines[r] = lines[r] - small[r][k] * lines[k]
                    for c in range(k + 1, STEP):
                        small[r][c] = small[r][c] - small[r][k] * small[k][c]
        for k in range(STEP):
            q = q - columns[k] * scaled[k]
        for k in range(STEP):
            q = jnp.where(rows == j + k, lines[k], q)
            signs = jnp.where(rows == j + k, chosen[k], signs)
    return q[:, B:], signs[:, :1]


def factor_values(gram, top):
    rows = lax.broadcasted_iota(jnp.int32, (B, 2 * B), 0)
    lanes = lax.broadcasted_iota(jnp.int32, (B, 2 * B), 1)
    small_rows = lax.broadcasted_iota(jnp.int32, (B, B), 0)
    small_lanes = lax.broadcasted_iota(jnp.int32, (B, B), 1)
    eye = jnp.where(small_rows == small_lanes, f32(1.0), f32(0.0))
    work = eliminate(jnp.concatenate([gram, eye], axis=1), rows)
    pivots = jnp.sum(jnp.where(rows == lanes, work, f32(0.0)), axis=1, keepdims=True)
    work = work * (1.0 / jnp.sqrt(pivots))
    upper = jnp.where(small_lanes >= small_rows, work[:, :B], f32(0.0))
    lower_inverse = work[:, B:]
    basis = product_nt(top, lower_inverse)
    inverse, signs = sign_inverse(jnp.concatenate([basis, eye], axis=1), rows)
    factor = -product_tn(lower_inverse, product(signs * inverse.T, lower_inverse))
    return factor, (signs * upper).T


def remote(src, dst, send_sem, recv_sem, device):
    return pltpu.make_async_remote_copy(
        src_ref=src,
        dst_ref=dst,
        send_sem=send_sem,
        recv_sem=recv_sem,
        device_id=device,
        device_id_type=MESH,
    )


def front_kernel(
    height, breadth, matrix, block, left, right,
    slab, strip, pc, pr, halves, own, parts, stats, chained, zs, rs, wr, wc, pe, ps, pt,
    local_sems, block_sems, pc_recvs, ring_sends, mate_sends, pr_recvs, pr_sends, part_sends, part_recvs,
    stat_sends, stat_recv, chain_send, chain_recv, rs_sends, rs_recvs, wr_right, wr_left, wr_recvs,
    role_send, wc_recvs, wc_sends, pe_sends, pe_recvs, pt_sends, pt_recvs,
):
    r, c = lax.axis_index("row"), lax.axis_index("col")
    rows, cols = matrix.shape
    width = cols // height
    half = height // 2
    count = height * breadth
    me = r * breadth + c
    core = lax.rem(r, 2)
    chip = r // 2
    even = core == 0
    odd = core == 1
    mate = r + 1 - 2 * core
    place = 2 * (chip // 2) + lax.rem(lax.rem(chip, 2) + chip // 2, 2)

    def seat(q):
        return 2 * (2 * (q // 2) + lax.rem(q + q // 2, 2))

    root = r == 0
    edge = c == 0

    slab_copy = pltpu.make_async_copy(matrix.at[pl.ds(0, B)], slab, local_sems.at[0])
    strip_copy = pltpu.make_async_copy(matrix.at[:, pl.ds(0, 2 * B)], strip, local_sems.at[1])
    pl.when(root)(slab_copy.start)
    pl.when(edge)(strip_copy.start)
    block_copies = []
    for k in range(breadth):
        part = pl.ds(k * width, width)
        block_copies.append(pltpu.make_async_copy(matrix.at[part], block.at[part], block_sems.at[k]))

    barrier = pltpu.get_barrier_semaphore()

    def greet(step, carry):
        other = lax.rem(me + step, count)
        pl.semaphore_signal(
            barrier, inc=1, device_id=(other // breadth, lax.rem(other, breadth)), device_id_type=MESH
        )
        return carry

    lax.fori_loop(1, count, greet, 0)

    def masked_slab():
        lane = lax.broadcasted_iota(jnp.int32, (B, cols), 1) + c * cols
        return jnp.where(lane >= B, slab[...], f32(0.0))

    @pl.when(root)
    def _():
        slab_copy.wait()
        panel = masked_slab()
        for i in range(height):
            pc[i] = panel[:, i * width : (i + 1) * width]

    pl.when(edge)(strip_copy.wait)
    for copy in block_copies:
        copy.start()

    @pl.when(root)
    def _():
        panel = masked_slab()
        top = jnp.where(edge, slab[:, B : 2 * B], f32(0.0))
        own[...] = jnp.concatenate([product_nt(panel, panel), top], axis=1)

    @pl.when(edge)
    def _():
        for k in range(breadth):
            piece = strip[k * width : (k + 1) * width, :].T[:B, :]
            lane = lax.broadcasted_iota(jnp.int32, (B, width), 1) + r * rows + k * width
            pr[k] = jnp.where(lane >= B, piece, f32(0.0))

    pl.semaphore_wait(barrier, count - 1)

    def piece_copy(i, part, sends, target):
        some = pc.at[i, pl.ds(part * (B // 2), B // 2)]
        return remote(some, some, sends.at[i, part], pc_recvs.at[i, part], (target, c))

    def ring_copy(i, part, target):
        return piece_copy(i, part, ring_sends, target)

    def mate_copy(i, part):
        return piece_copy(i, part, mate_sends, mate)

    def part_copy(k):
        return remote(own, parts.at[c], part_sends.at[k], part_recvs.at[c], (1, k))

    forth = seat(lax.rem(place + 1, half))
    back = seat(lax.rem(place + half - 1, half))
    goes_forth = place + 1 < half
    goes_back = place != 1

    def ring_on(i, part):
        if i < half:
            pl.when(goes_forth)(ring_copy(i, part, forth).start)
        else:
            pl.when(goes_back)(ring_copy(i, part, back).start)

    def passed(i, part):
        mate_copy(i, part).wait_recv()
        ring_on(i, part)
        mate_copy(i, part).start()

    @pl.when(root)
    def _():
        for k in range(breadth):
            part_copy(k).start()
        for i in range(half):
            for part in range(2):
                ring_copy(i, part, forth).start()
                ring_copy(half + i, part, back).start()
        for i in range(height):
            for part in range(2):
                mate_copy(i, part).start()

    def line_copy(k):
        return remote(pr.at[k], pr.at[k], pr_sends.at[k], pr_recvs.at[k], (r, c + 1))

    def line_received(k):
        remote(pr.at[k], pr.at[k], pr_sends.at[k], pr_recvs.at[k], (r, 0)).wait_recv()

    @pl.when(edge)
    def _():
        for k in range(breadth - 1, -1, -1):
            line_copy(k).start()

    middle = jnp.logical_and(c >= 1, c < breadth - 1)

    def line_pass(who, index, when=True):
        k = breadth - 1 - index

        @pl.when(jnp.logical_and(jnp.logical_and(middle, c == who), when))
        def _():
            line_received(k)
            line_copy(k).start()

    relays = jnp.logical_and(even, jnp.logical_not(root))

    def go_round(pieces):
        for step, (i, part) in enumerate(pieces):
            passed(i, part)
            for index in range(breadth):
                if (index + 1) * len(pieces) // breadth - 1 == step:
                    line_pass(1, index)

    pieces = [(i, part) for i in range(height) for part in range(2)]
    later = pieces[height:] + pieces[:height]

    @pl.when(jnp.logical_and(relays, 2 * place < half))
    def _():
        go_round(pieces)

    @pl.when(jnp.logical_and(relays, 2 * place == half))
    def _():
        go_round([piece for pair in zip(pieces[:height], later[:height]) for piece in pair])

    @pl.when(jnp.logical_and(relays, 2 * place > half))
    def _():
        go_round(later)

    @pl.when(root)
    def _():
        for index in range(breadth):
            line_pass(1, index)

    def stat_copy(q):
        return remote(stats, stats, stat_sends.at[q], stat_recv, (2 * q + 1, c))

    chain_copy = remote(chained, chained, chain_send, chain_recv, (mate, c))

    @pl.when(r == 1)
    def _():
        total = None
        for k in range(breadth):
            remote(parts.at[k], parts.at[k], part_sends.at[k], part_recvs.at[k], (0, c)).wait_recv()
            total = parts[k] if total is None else total + parts[k]
        stats[...] = total
        for q in range(1, half):
            stat_copy(q).start()

    pl.when(odd)(lambda: line_pass(1, 0))

    @pl.when(jnp.logical_and(odd, r != 1))
    def _():
        remote(stats, stats, stat_sends.at[0], stat_recv, (1, c)).wait_recv()

    @pl.when(odd)
    def _():
        factor, turned = factor_values(stats[:, :B], stats[:, B:].T)
        chained[...] = jnp.concatenate([factor, turned], axis=1)
        chain_copy.start()
        for index in range(1, breadth):
            line_pass(1, index)
        for i, part in pieces:
            mate_copy(i, part).wait_recv()

    @pl.when(even)
    def _():
        for i, part in pieces:
            mate_copy(i, part).wait_send()
        chain_copy.wait_recv()

    @pl.when(root)
    def _():
        for i, part in pieces[:height]:
            ring_copy(i, part, forth).wait_send()
            ring_copy(half + i, part, back).wait_send()

    @pl.when(relays)
    def _():
        for i, part in pieces[:height]:
            pl.when(goes_forth)(ring_copy(i, part, forth).wait_send)
            pl.when(goes_back)(ring_copy(half + i, part, back).wait_send)

    def lower_top(buffer):
        for i in range(buffer.shape[0]):
            low, high = max(B, i * width), min(2 * B, (i + 1) * width)
            if low < high:
                lanes = slice(low - i * width, high - i * width)
                buffer[i, :, lanes] = buffer[i, :, lanes] - chained[:, low : high]

    @pl.when(edge)
    def _():
        lower_top(pc)

    for i in range(height):
        part = slice(i * width, (i + 1) * width)
        upper, lower = split(pc[i])
        halves[:B, part] = upper
        halves[B:, part] = lower
    for copy in block_copies:
        copy.wait()

    size = min(512, cols)

    def rs_copy(step, other):
        return remote(zs.at[other], rs.at[c], rs_sends.at[step], rs_recvs.at[c], (r, other))

    order = sorted(range(1, breadth), key=lambda s: -min(s, breadth - s)) + [0]
    for index, step in enumerate(order):
        for k in range(breadth):
            early = max(0, k - breadth // 4)
            late = min(breadth - 1, breadth - 2 + k // 2)
            if 4 * early // breadth == index:
                line_pass(2, k, r >= 2)
            if late == index:
                line_pass(2, k, r < 2)
        other = lax.rem(c + step, breadth)
        some = pl.ds(pl.multiple_of(other * width, width), width)
        both = jnp.zeros((width, 2 * B), f32)
        for start in range(0, cols, size):
            part = slice(start, start + size)
            upper, lower = split(block[some, part])
            both = both + lax.dot_general(upper, halves[:, part], NT, preferred_element_type=f32)
            low = lax.dot_general(lower, halves[:, part], NT, preferred_element_type=f32)
            both = both + jnp.where(lax.broadcasted_iota(jnp.int32, both.shape, 1) < B, low, f32(0.0))
        turned = both.T
        value = turned[:B, :] + turned[B:, :]
        if step:
            zs[other] = value
            rs_copy(step, other).start()
        else:
            rs[c] = value
    for who in range(3, breadth - 1):
        for k in range(breadth):
            line_pass(who, k)

    for step in range(1, breadth):
        other = lax.rem(c + step, breadth)
        remote(rs.at[other], rs.at[other], rs_sends.at[step], rs_recvs.at[other], (r, other)).wait_recv()
    total = rs[0]
    for k in range(1, breadth):
        total = total + rs[k]
    wr[c] = total

    def sum_copy(k, part, sends, target):
        some = wr.at[k, pl.ds(part * (B // 2), B // 2)]
        return remote(some, some, sends.at[k, part], wr_recvs.at[k, part], (r, target))

    def right_copy(k, part):
        return sum_copy(k, part, wr_right, c + 1)

    def left_copy(k, part):
        return sum_copy(k, part, wr_left, c - 1)

    has_right = c + 1 < breadth
    has_left = c >= 1
    to_row = lax.rem(me, height)
    to_col = me // height
    itself = jnp.logical_and(to_row == r, to_col == c)
    role = remote(wr.at[c], wc.at[to_row], role_send, wc_recvs.at[to_row], (to_row, to_col))
    pl.when(jnp.logical_not(itself))(role.start)
    for part in range(2):
        pl.when(has_right)(right_copy(c, part).start)
        pl.when(has_left)(left_copy(c, part).start)

    @pl.when(itself)
    def _():
        wc[r] = total

    @pl.when(c == breadth - 1)
    def _():
        line_received(breadth - 1)

    slots = lax.broadcasted_iota(jnp.int32, (B, width), 0)
    positions = lax.broadcasted_iota(jnp.int32, (B, width), 1) + me * width - B
    onehot = jnp.where(positions == slots, f32(1.0), f32(0.0))
    vector = pr[c] - product(chained[:, B:], onehot)
    pe[r] = jnp.concatenate([product_nt(total, vector), jnp.zeros((B, B), f32)], axis=1)

    def pe_copy(step):
        other = lax.rem(r + step, height)
        return remote(pe.at[r], pe.at[r], pe_sends.at[step], pe_recvs.at[r], (other, c)), other

    for step in range(1, height):
        pe_copy(step)[0].start()

    def wr_pass(s):
        for part in range(2):

            @pl.when(c - s >= 0)
            def _():
                sum_copy(c - s, part, wr_right, c - 1).wait_recv()
                pl.when(has_right)(right_copy(c - s, part).start)

            @pl.when(c + s < breadth)
            def _():
                sum_copy(c + s, part, wr_left, c + 1).wait_recv()
                pl.when(has_left)(left_copy(c + s, part).start)

    def wc_copy(slot, step, other):
        return remote(wc.at[slot], wc.at[slot], wc_sends.at[step], wc_recvs.at[slot], (other, c))

    def wc_received(slot):
        remote(wc.at[slot], wc.at[slot], wc_sends.at[0], wc_recvs.at[slot], (mate, c)).wait_recv()

    pl.when(jnp.logical_not(itself))(lambda: wc_received(r))
    for step in range(2, height, 2):
        wc_copy(r, step, lax.rem(r + step, height)).start()
    wc_copy(r, 1, mate).start()
    wr_pass(1)
    summed = pe[r]
    for step in range(1, height):
        copy, other = pe_copy(step)
        remote(pe.at[other], pe.at[other], pe_sends.at[step], pe_recvs.at[other], (other, c)).wait_recv()
        summed = summed + pe[other]
    ps[c] = summed

    def ps_copy(step):
        other = lax.rem(c + step, breadth)
        return remote(ps.at[c], ps.at[c], pt_sends.at[step], pt_recvs.at[c], (r, other)), other

    for step in range(1, breadth):
        ps_copy(step)[0].start()
    for s in range(2, breadth - 1):
        wr_pass(s)
    for step in range(2, height, 2):
        slot = lax.rem(r + step, height)
        wc_received(slot)
        wc_copy(slot, step + 1, mate).start()
    if breadth > 2:
        wr_pass(breadth - 1)
    projected = ps[c]
    for step in range(1, breadth):
        copy, other = ps_copy(step)
        remote(ps.at[other], ps.at[other], pt_sends.at[step], pt_recvs.at[other], (r, other)).wait_recv()
        projected = projected + ps[other]

    factor = chained[:, :B]
    turned = factor.T
    inner = product(turned, product(projected[:, :B], factor))
    mix = jnp.concatenate([turned, -0.5 * inner], axis=1)
    wc_received(mate)
    for step in range(2, height, 2):
        wc_received(lax.rem(mate + step, height))
    for i in range(height):
        part = slice(i * width, (i + 1) * width)
        v = pc[i]
        u = product(mix, jnp.concatenate([wc[i], v], axis=0))
        upper, lower = split(jnp.concatenate([u, v], axis=0))
        right[: 2 * B, part] = upper
        right[2 * B : 4 * B, part] = upper
        right[4 * B :, part] = lower

    @pl.when(c == breadth - 1)
    def _():
        for k in range(breadth - 1):
            line_received(k)

    @pl.when(c < breadth - 1)
    def _():
        for k in range(breadth):
            line_copy(k).wait_send()

    @pl.when(root)
    def _():
        lower_top(pr)

    for i in range(breadth):
        part = slice(i * width, (i + 1) * width)
        v = pr[i]
        u = product(mix, jnp.concatenate([wr[i], v], axis=0))
        upper, lower = split(jnp.concatenate([v, u], axis=0).T)
        left[part, : 2 * B] = upper
        left[part, 2 * B : 4 * B] = lower
        left[part, 4 * B :] = upper

    @pl.when(root)
    def _():
        for k in range(breadth):
            part_copy(k).wait_send()

    @pl.when(r == 1)
    def _():
        for q in range(1, half):
            stat_copy(q).wait_send()

    pl.when(odd)(chain_copy.wait_send)
    for step in range(1, breadth):
        rs_copy(step, lax.rem(c + step, breadth)).wait_send()
        ps_copy(step)[0].wait_send()
    for step in range(1, height):
        pe_copy(step)[0].wait_send()
    pl.when(jnp.logical_not(itself))(role.wait_send)
    for step in range(2, height, 2):
        wc_copy(r, step, lax.rem(r + step, height)).wait_send()
        wc_copy(lax.rem(r + step, height), step + 1, mate).wait_send()
    wc_copy(r, 1, mate).wait_send()

    @pl.when(has_right)
    def _():
        for k in range(breadth):
            for part in range(2):
                pl.when(k <= c)(right_copy(k, part).wait_send)

    @pl.when(has_left)
    def _():
        for k in range(breadth):
            for part in range(2):
                pl.when(k >= c)(left_copy(k, part).wait_send)


def front(matrix, height, breadth):
    rows, cols = matrix.shape
    width = cols // height
    vmem = pl.BlockSpec(memory_space=pltpu.VMEM)
    dma = pltpu.SemaphoreType.DMA
    scratch = [
        pltpu.VMEM((B, cols), f32),
        pltpu.VMEM((rows, 2 * B), f32),
        pltpu.VMEM((height, B, width), f32),
        pltpu.VMEM((breadth, B, width), f32),
        pltpu.VMEM((2 * B, cols), bf16),
        pltpu.VMEM((B, 2 * B), f32),
        pltpu.VMEM((breadth, B, 2 * B), f32),
        pltpu.VMEM((B, 2 * B), f32),
        pltpu.VMEM((B, 2 * B), f32),
        pltpu.VMEM((breadth, B, width), f32),
        pltpu.VMEM((breadth, B, width), f32),
        pltpu.VMEM((breadth, B, width), f32),
        pltpu.VMEM((height, B, width), f32),
        pltpu.VMEM((height, B, 2 * B), f32),
        pltpu.VMEM((breadth, B, 2 * B), f32),
        pltpu.VMEM((B, 2 * B), f32),
        dma((2,)),
        dma((breadth,)),
        dma((height, 2)),
        dma((height, 2)),
        dma((height, 2)),
        dma((breadth,)),
        dma((breadth,)),
        dma((breadth,)),
        dma((breadth,)),
        dma((height // 2,)),
        dma(()),
        dma(()),
        dma(()),
        dma((breadth,)),
        dma((breadth,)),
        dma((breadth, 2)),
        dma((breadth, 2)),
        dma((breadth, 2)),
        dma(()),
        dma((height,)),
        dma((height,)),
        dma((height,)),
        dma((height,)),
        dma((breadth,)),
        dma((breadth,)),
    ]
    return pl.pallas_call(
        lambda *refs: front_kernel(height, breadth, *refs),
        out_shape=[
            pltpu.VMEM((rows, cols), f32),
            pltpu.VMEM((rows, 6 * B), bf16),
            pltpu.VMEM((6 * B, cols), bf16),
        ],
        in_specs=[pl.BlockSpec(memory_space=pl.ANY)],
        out_specs=[vmem] * 3,
        scratch_shapes=scratch,
        compiler_params=pltpu.CompilerParams(
            collective_id=0, has_side_effects=True, vmem_limit_bytes=20 << 20
        ),
        name="front",
    )(matrix)


def final_kernel(tile, slots, block, left, right, out, buffer, sems):
    rows, cols = block.shape
    size = min(512, cols)
    count = rows // tile

    def copy(i):
        return pltpu.make_async_copy(
            buffer.at[i % slots], out.at[pl.ds(i * tile, tile)], sems.at[i % slots]
        )

    for i in range(count):
        if i >= slots:
            copy(i - slots).wait()
        some = slice(i * tile, (i + 1) * tile)
        for start in range(0, cols, size):
            part = slice(start, start + size)
            buffer[i % slots, :, part] = block[some, part] - jnp.dot(
                left[some, :], right[:, part], preferred_element_type=f32
            )
        copy(i).start()
    for i in range(max(0, count - slots), count):
        copy(i).wait()


def final(block, left, right):
    rows, cols = block.shape
    tile = min(256, rows)
    slots = min(4, rows // tile)
    vmem = pl.BlockSpec(memory_space=pltpu.VMEM)
    held = [pltpu.with_memory_space_constraint(x, pltpu.VMEM) for x in (block, left, right)]
    return pl.pallas_call(
        lambda *refs: final_kernel(tile, slots, *refs),
        out_shape=jax.ShapeDtypeStruct((rows, cols), f32),
        in_specs=[vmem] * 3,
        out_specs=pl.BlockSpec(memory_space=pl.ANY),
        scratch_shapes=[
            pltpu.VMEM((slots, tile, cols), f32),
            pltpu.SemaphoreType.DMA((slots,)),
        ],
        compiler_params=pltpu.CompilerParams(vmem_limit_bytes=20 << 20),
        name="final",
    )(*held)


def solution(mesh):
    height, breadth = mesh.shape["row"], mesh.shape["col"]

    def shards(matrix):
        return final(*front(matrix, height, breadth))

    return jax.shard_map(
        shards,
        mesh=mesh,
        in_specs=(P("row", "col"),),
        out_specs=P("row", "col"),
        check_vma=False,
    )
```

```python
import jax
import jax.numpy as jnp
from jax import lax
from jax.experimental import pallas as pl
from jax.experimental.pallas import tpu as pltpu
from jax.sharding import PartitionSpec as P

B = 64
STEP = 8


highest = lax.Precision.HIGHEST
MESH = pl.DeviceIdType.MESH
f32 = jnp.float32
bf16 = jnp.bfloat16
NT = (((1,), (1,)), ((), ()))
TN = (((0,), (0,)), ((), ()))


def product(left, right):
    return jnp.dot(left, right, precision=highest, preferred_element_type=f32)


def product_nt(left, right):
    return lax.dot_general(left, right, NT, precision=highest, preferred_element_type=f32)


def product_tn(left, right):
    return lax.dot_general(left, right, TN, precision=highest, preferred_element_type=f32)


def split(x):
    upper = x.astype(bf16)
    return upper, (x - upper.astype(f32)).astype(bf16)


def product_halves(left, right):
    upper, lower = split(right)
    return jnp.dot(left, jnp.concatenate([upper, upper, lower], axis=0), preferred_element_type=f32)


def eliminate(work, rows):
    for j in range(0, B, STEP):
        columns = [jnp.broadcast_to(work[:, j + k : j + k + 1], work.shape) for k in range(STEP)]
        lines = [work[j + k : j + k + 1, :] for k in range(STEP)]
        small = [[columns[c][j + r : j + r + 1, :] for c in range(STEP)] for r in range(STEP)]
        scaled = []
        for k in range(STEP):
            inverse = 1.0 / small[k][k]
            scaled.append(lines[k] * inverse)
            for m in range(k + 1, STEP):
                ratio = small[k][m] * inverse
                columns[m] = columns[m] - columns[k] * ratio
                lines[m] = lines[m] - lines[k] * ratio
                for c in range(m, STEP):
                    small[m][c] = small[m][c] - ratio * small[k][c]
        lowered = work
        for k in range(STEP):
            lowered = lowered - columns[k] * scaled[k]
        lowered = jnp.where(rows >= j + STEP, lowered, work)
        for k in range(1, STEP):
            lowered = jnp.where(rows == j + k, lines[k], lowered)
        work = lowered
    return work


def sign_inverse(q, rows):
    lane = lax.broadcasted_iota(jnp.int32, (1, 2 * B), 1)
    signs = jnp.zeros((B, 2 * B), f32)
    for j in range(0, B, STEP):
        columns = [jnp.broadcast_to(q[:, j + k : j + k + 1], q.shape) for k in range(STEP)]
        lines = [q[j + k : j + k + 1, :] for k in range(STEP)]
        small = [[columns[c][j + r : j + r + 1, :] for c in range(STEP)] for r in range(STEP)]
        scaled = []
        chosen = []
        for k in range(STEP):
            sign = jnp.where(small[k][k] >= 0, f32(-1.0), f32(1.0))
            pivot = small[k][k] - sign
            inverse = 1.0 / pivot
            chosen.append(sign)
            lines[k] = jnp.where(lane == j + k, pivot, lines[k]) * inverse
            scaled.append(lines[k])
            for c in range(k + 1, STEP):
                small[k][c] = small[k][c] * inverse
                columns[c] = columns[c] - columns[k] * small[k][c]
            for r in range(STEP):
                if r != k:
                    lines[r] = lines[r] - small[r][k] * lines[k]
                    for c in range(k + 1, STEP):
                        small[r][c] = small[r][c] - small[r][k] * small[k][c]
        for k in range(STEP):
            q = q - columns[k] * scaled[k]
        for k in range(STEP):
            q = jnp.where(rows == j + k, lines[k], q)
            signs = jnp.where(rows == j + k, chosen[k], signs)
    return q[:, B:], signs[:, :1]


def factor_values(gram, top):
    rows = lax.broadcasted_iota(jnp.int32, (B, 2 * B), 0)
    lanes = lax.broadcasted_iota(jnp.int32, (B, 2 * B), 1)
    small_rows = lax.broadcasted_iota(jnp.int32, (B, B), 0)
    small_lanes = lax.broadcasted_iota(jnp.int32, (B, B), 1)
    eye = jnp.where(small_rows == small_lanes, f32(1.0), f32(0.0))
    work = eliminate(jnp.concatenate([gram, eye], axis=1), rows)
    pivots = jnp.sum(jnp.where(rows == lanes, work, f32(0.0)), axis=1, keepdims=True)
    work = work * (1.0 / jnp.sqrt(pivots))
    upper = jnp.where(small_lanes >= small_rows, work[:, :B], f32(0.0))
    lower_inverse = work[:, B:]
    basis = product_nt(top, lower_inverse)
    inverse, signs = sign_inverse(jnp.concatenate([basis, eye], axis=1), rows)
    factor = -product_tn(lower_inverse, product(signs * inverse.T, lower_inverse))
    return factor, (signs * upper).T


def remote(src, dst, send_sem, recv_sem, device):
    return pltpu.make_async_remote_copy(
        src_ref=src,
        dst_ref=dst,
        send_sem=send_sem,
        recv_sem=recv_sem,
        device_id=device,
        device_id_type=MESH,
    )


def front_kernel(
    height, breadth, matrix, block, right, pr, wr, mix,
    slab, strip, pc, halves, own, parts, stats, chained, zs, near, rs, wc, pe, ps,
    local_sems, block_sems, pc_recvs, ring_sends, mate_sends, pr_recvs, pr_sends, part_sends, part_recvs,
    stat_sends, stat_recv, chain_send, chain_recv, raw_sends, near_recvs, rs_sends, rs_recvs, wr_right, wr_left, wr_recvs,
    role_send, wc_recvs, wc_sends, pe_sends, pe_recvs, pt_sends, pt_recvs,
):
    r, c = lax.axis_index("row"), lax.axis_index("col")
    rows, cols = matrix.shape
    width = cols // height
    half = height // 2
    count = height * breadth
    me = r * breadth + c
    core = lax.rem(r, 2)
    chip = r // 2
    even = core == 0
    odd = core == 1
    mate = r + 1 - 2 * core
    place = 2 * (chip // 2) + lax.rem(lax.rem(chip, 2) + chip // 2, 2)

    def seat(q):
        return 2 * (2 * (q // 2) + lax.rem(q + q // 2, 2))

    root = r == 0
    edge = c == 0
    home = r // (height // breadth)
    low_home = home == 0
    high_home = home == breadth - 1
    at_home = jnp.logical_and(high_home, c == breadth - 1)
    reach = jnp.where(high_home, breadth - 2, breadth - 1)

    slab_copy = pltpu.make_async_copy(matrix.at[pl.ds(0, B)], slab, local_sems.at[0])
    strip_copy = pltpu.make_async_copy(matrix.at[:, pl.ds(0, 2 * B)], strip, local_sems.at[1])
    pl.when(root)(slab_copy.start)
    pl.when(edge)(strip_copy.start)
    block_copies = []
    for k in range(breadth):
        part = pl.ds(k * width, width)
        block_copies.append(pltpu.make_async_copy(matrix.at[part], block.at[part], block_sems.at[k]))

    barrier = pltpu.get_barrier_semaphore()

    def greet(step, carry):
        other = lax.rem(me + step, count)
        pl.semaphore_signal(
            barrier, inc=1, device_id=(other // breadth, lax.rem(other, breadth)), device_id_type=MESH
        )
        return carry

    lax.fori_loop(1, count, greet, 0)

    def masked_slab():
        lane = lax.broadcasted_iota(jnp.int32, (B, cols), 1) + c * cols
        return jnp.where(lane >= B, slab[...], f32(0.0))

    @pl.when(root)
    def _():
        slab_copy.wait()
        panel = masked_slab()
        for i in range(height):
            pc[i] = panel[:, i * width : (i + 1) * width]

    pl.when(edge)(strip_copy.wait)
    for copy in block_copies:
        copy.start()

    @pl.when(root)
    def _():
        panel = masked_slab()
        top = jnp.where(edge, slab[:, B : 2 * B], f32(0.0))
        own[...] = jnp.concatenate([product_nt(panel, panel), top], axis=1)

    @pl.when(edge)
    def _():
        for k in range(breadth):
            piece = strip[k * width : (k + 1) * width, :].T[:B, :]
            lane = lax.broadcasted_iota(jnp.int32, (B, width), 1) + r * rows + k * width
            pr[k] = jnp.where(lane >= B, piece, f32(0.0))

    pl.semaphore_wait(barrier, count - 1)

    def piece_copy(i, part, sends, target):
        some = pc.at[i, pl.ds(part * (B // 2), B // 2)]
        return remote(some, some, sends.at[i, part], pc_recvs.at[i, part], (target, c))

    def ring_copy(i, part, target):
        return piece_copy(i, part, ring_sends, target)

    def mate_copy(i, part):
        return piece_copy(i, part, mate_sends, mate)

    def part_copy(k):
        return remote(own, parts.at[c], part_sends.at[k], part_recvs.at[c], (1, k))

    forth = seat(lax.rem(place + 1, half))
    back = seat(lax.rem(place + half - 1, half))
    goes_forth = place + 1 < half
    goes_back = place != 1

    def ring_on(i, part):
        if i < half:
            pl.when(goes_forth)(ring_copy(i, part, forth).start)
        else:
            pl.when(goes_back)(ring_copy(i, part, back).start)

    def passed(i, part):
        mate_copy(i, part).wait_recv()
        ring_on(i, part)
        mate_copy(i, part).start()

    @pl.when(root)
    def _():
        for k in range(breadth):
            part_copy(k).start()
        for i in range(half):
            for part in range(2):
                ring_copy(i, part, forth).start()
                ring_copy(half + i, part, back).start()

    def line_copy(k):
        return remote(pr.at[k], pr.at[k], pr_sends.at[k], pr_recvs.at[k], (r, c + 1))

    def line_received(k):
        remote(pr.at[k], pr.at[k], pr_sends.at[k], pr_recvs.at[k], (r, 0)).wait_recv()

    @pl.when(edge)
    def _():
        for k in range(breadth - 1, -1, -1):
            line_copy(k).start()

    middle = jnp.logical_and(c >= 1, c < reach)

    def line_pass(who, index, when=True):
        k = breadth - 1 - index

        @pl.when(jnp.logical_and(jnp.logical_and(middle, c == who), when))
        def _():
            line_received(k)
            line_copy(k).start()

    relays = jnp.logical_and(even, jnp.logical_not(root))

    def halve(i):
        some = slice(i * width, (i + 1) * width)
        upper, lower = split(pc[i])
        halves[:B, some] = upper
        halves[B:, some] = lower

    def go_round(pieces):
        for step, (i, part) in enumerate(pieces):
            passed(i, part)
            if part:
                halve(i)
            for index in range(breadth):
                if (index + 1) * len(pieces) // breadth - 1 == step:
                    line_pass(1, index)

    pieces = [(i, part) for i in range(height) for part in range(2)]
    later = pieces[height:] + pieces[:height]

    @pl.when(jnp.logical_and(relays, 2 * place < half))
    def _():
        go_round(pieces)

    @pl.when(jnp.logical_and(relays, 2 * place == half))
    def _():
        go_round([piece for pair in zip(pieces[:height], later[:height]) for piece in pair])

    @pl.when(jnp.logical_and(relays, 2 * place > half))
    def _():
        go_round(later)

    @pl.when(root)
    def _():
        for i, part in pieces[:height]:
            ring_copy(i, part, forth).wait_send()
            ring_copy(half + i, part, back).wait_send()
        for i, part in pieces:
            mate_copy(i, part).start()
        for i in range(height):
            halve(i)
        for index in range(breadth):
            line_pass(1, index)

    def stat_copy(q):
        return remote(stats, stats, stat_sends.at[q], stat_recv, (2 * q + 1, c))

    chain_copy = remote(chained, chained, chain_send, chain_recv, (mate, c))

    @pl.when(r == 1)
    def _():
        total = None
        for k in range(breadth):
            remote(parts.at[k], parts.at[k], part_sends.at[k], part_recvs.at[k], (0, c)).wait_recv()
            total = parts[k] if total is None else total + parts[k]
        stats[...] = total
        for q in range(1, half):
            stat_copy(q).start()

    pl.when(odd)(lambda: line_pass(1, 0))

    @pl.when(jnp.logical_and(odd, r != 1))
    def _():
        remote(stats, stats, stat_sends.at[0], stat_recv, (1, c)).wait_recv()

    @pl.when(odd)
    def _():
        factor, turned = factor_values(stats[:, :B], stats[:, B:].T)
        chained[...] = jnp.concatenate([factor, turned], axis=1)
        chain_copy.start()
        for index in range(1, breadth):
            line_pass(1, index)
        for i, part in pieces:
            mate_copy(i, part).wait_recv()
            if part:
                halve(i)

    @pl.when(even)
    def _():
        for i, part in pieces:
            mate_copy(i, part).wait_send()
        chain_copy.wait_recv()

    @pl.when(relays)
    def _():
        for i, part in pieces[:height]:
            pl.when(goes_forth)(ring_copy(i, part, forth).wait_send)
            pl.when(goes_back)(ring_copy(half + i, part, back).wait_send)

    def lower_top(buffer):
        for i in range(buffer.shape[0]):
            low, high = max(B, i * width), min(2 * B, (i + 1) * width)
            if low < high:
                lanes = slice(low - i * width, high - i * width)
                buffer[i, :, lanes] = buffer[i, :, lanes] - chained[:, low : high]

    @pl.when(edge)
    def _():
        lower_top(pc)
        for i in range(height):
            if max(B, i * width) < min(2 * B, (i + 1) * width):
                halve(i)

    @pl.when(at_home)
    def _():
        for k in range(breadth):
            pr[k] = pc[lax.rem(r * breadth + k, height)]

    for copy in block_copies:
        copy.wait()

    size = min(512, cols)

    pair = c // 2
    late = lax.rem(c, 2)
    friend = c + 1 - 2 * late
    pairs = breadth // 2

    def raw_copy(index, k):
        return remote(zs.at[k], near.at[k], raw_sends.at[index], near_recvs.at[k], (r, friend))

    def sum_of_pair(index, k):
        return remote(zs.at[k], rs.at[pair], rs_sends.at[index], rs_recvs.at[pair], (r, k))

    def chunk_at(index):
        if index < breadth - 2:
            whose = lax.rem(pair + 1 + index // 2, pairs)
            above = jnp.where(whose > pair, 1, 0)
            first = jnp.where(whose > pair, 1 - index % 2, index % 2)
            return 2 * whose + first, above == late
        return (friend if index == breadth - 2 else c), None

    def add_pair(index):
        k, adds = chunk_at(index)

        @pl.when(adds)
        def _():
            raw_copy(index, k).wait_recv()
            zs[k] = zs[k] + near[k]
            sum_of_pair(index, k).start()

    for index in range(breadth):
        if index in (0, breadth // 2):
            for k in range(breadth // 2):
                line_pass(2, k, (r >= 2) if index == 0 else (r < 2))
        other, adds = chunk_at(index)
        some = pl.ds(pl.multiple_of(other * width, width), width)
        both = jnp.zeros((width, 2 * B), f32)
        for start in range(0, cols, size):
            part = slice(start, start + size)
            upper, lower = split(block[some, part])
            both = both + lax.dot_general(upper, halves[:, part], NT, preferred_element_type=f32)
            low = lax.dot_general(lower, halves[:, part], NT, preferred_element_type=f32)
            both = both + jnp.where(lax.broadcasted_iota(jnp.int32, both.shape, 1) < B, low, f32(0.0))
        turned = both.T
        value = turned[:B, :] + turned[B:, :]
        zs[other] = value
        if index < breadth - 2:
            pl.when(jnp.logical_not(adds))(raw_copy(index, other).start)
        elif index == breadth - 2:
            raw_copy(index, other).start()
        if index >= 2:
            add_pair(index - 2)
    for k in range(breadth // 2, breadth):
        line_pass(2, k)
    for who in range(3, breadth - 1):
        for k in range(breadth):
            line_pass(who, k)

    raw_copy(0, c).wait_recv()
    total = zs[c] + near[c]
    for step in range(1, pairs):
        other = lax.rem(pair + step, pairs)
        remote(rs.at[other], rs.at[other], rs_sends.at[0], rs_recvs.at[other], (r, friend)).wait_recv()
        total = total + rs[other]
    wr[c] = total

    def sum_copy(k, part, sends, target):
        some = wr.at[k, pl.ds(part * (B // 2), B // 2)]
        return remote(some, some, sends.at[k, part], wr_recvs.at[k, part], (r, target))

    def right_copy(k, part):
        return sum_copy(k, part, wr_right, c + 1)

    def left_copy(k, part):
        return sum_copy(k, part, wr_left, c - 1)

    has_right = jnp.logical_and(c + 1 < breadth, jnp.logical_not(jnp.logical_and(high_home, c == breadth - 2)))
    has_left = jnp.logical_and(c >= 1, jnp.logical_not(jnp.logical_and(low_home, c == 1)))
    takes_right = jnp.logical_not(jnp.logical_and(low_home, edge))
    takes_left = jnp.logical_not(jnp.logical_and(high_home, c == breadth - 1))
    to_row = lax.rem(me, height)
    to_col = me // height
    itself = jnp.logical_and(to_row == r, to_col == c)
    role = remote(wr.at[c], wc.at[to_row], role_send, wc_recvs.at[to_row], (to_row, to_col))
    pl.when(jnp.logical_not(itself))(role.start)
    for part in range(2):
        pl.when(has_right)(right_copy(c, part).start)
        pl.when(has_left)(left_copy(c, part).start)

    @pl.when(itself)
    def _():
        wc[r] = total

    @pl.when(c == reach)
    def _():
        line_received(c)

    slots = lax.broadcasted_iota(jnp.int32, (B, width), 0)
    positions = lax.broadcasted_iota(jnp.int32, (B, width), 1) + me * width - B
    onehot = jnp.where(positions == slots, f32(1.0), f32(0.0))
    vector = pr[c] - product(chained[:, B:], onehot)
    pe[r] = jnp.concatenate([product_nt(total, vector), jnp.zeros((B, B), f32)], axis=1)

    def pe_copy(step):
        other = lax.rem(r + step, height)
        return remote(pe.at[r], pe.at[r], pe_sends.at[step], pe_recvs.at[r], (other, c)), other

    for step in range(1, height):
        pe_copy(step)[0].start()

    def wr_pass(s):
        for part in range(2):

            @pl.when(jnp.logical_and(c - s >= 0, takes_left))
            def _():
                sum_copy(c - s, part, wr_right, c - 1).wait_recv()
                pl.when(has_right)(right_copy(c - s, part).start)

            @pl.when(jnp.logical_and(c + s < breadth, takes_right))
            def _():
                sum_copy(c + s, part, wr_left, c + 1).wait_recv()
                pl.when(has_left)(left_copy(c + s, part).start)

    def wc_copy(slot, step, other):
        return remote(wc.at[slot], wc.at[slot], wc_sends.at[step], wc_recvs.at[slot], (other, c))

    def wc_received(slot):
        remote(wc.at[slot], wc.at[slot], wc_sends.at[0], wc_recvs.at[slot], (mate, c)).wait_recv()

    pl.when(jnp.logical_not(itself))(lambda: wc_received(r))
    for step in range(2, height, 2):
        wc_copy(r, step, lax.rem(r + step, height)).start()
    wc_copy(r, 1, mate).start()
    wr_pass(1)
    summed = pe[r]
    for step in range(1, height):
        copy, other = pe_copy(step)
        remote(pe.at[other], pe.at[other], pe_sends.at[step], pe_recvs.at[other], (other, c)).wait_recv()
        summed = summed + pe[other]
    ps[c] = summed

    def ps_copy(step):
        other = lax.rem(c + step, breadth)
        return remote(ps.at[c], ps.at[c], pt_sends.at[step], pt_recvs.at[c], (r, other)), other

    for step in range(1, breadth):
        ps_copy(step)[0].start()
    for s in range(2, breadth - 1):
        wr_pass(s)
    for step in range(2, height, 2):
        slot = lax.rem(r + step, height)
        wc_received(slot)
        wc_copy(slot, step + 1, mate).start()
    if breadth > 2:
        wr_pass(breadth - 1)
    projected = ps[c]
    for step in range(1, breadth):
        copy, other = ps_copy(step)
        remote(ps.at[other], ps.at[other], pt_sends.at[step], pt_recvs.at[other], (r, other)).wait_recv()
        projected = projected + ps[other]

    factor = chained[:, :B]
    turned = factor.T
    inner = product(turned, product(projected[:, :B], factor))
    upper, lower = split(jnp.concatenate([turned, -0.5 * inner], axis=1))
    mix[...] = jnp.concatenate([upper, lower, upper], axis=1)
    wc_received(mate)
    for step in range(2, height, 2):
        wc_received(lax.rem(mate + step, height))
    for i in range(height):
        part = slice(i * width, (i + 1) * width)
        v = pc[i]
        u = product_halves(mix[...], jnp.concatenate([wc[i], v], axis=0))
        upper, lower = split(jnp.concatenate([u, v], axis=0))
        right[: 2 * B, part] = upper
        right[2 * B : 4 * B, part] = upper
        right[4 * B :, part] = lower

    @pl.when(c == reach)
    def _():
        for k in range(breadth):
            pl.when(k != c)(lambda: line_received(k))

    @pl.when(c < reach)
    def _():
        for k in range(breadth):
            line_copy(k).wait_send()

    @pl.when(root)
    def _():
        lower_top(pr)

    @pl.when(jnp.logical_not(jnp.logical_and(takes_left, takes_right)))
    def _():
        for k in range(breadth):

            @pl.when(k != c)
            def _():
                wr[k] = wc[lax.rem(r * breadth + k, height)]

    for index in range(breadth - 1):
        k, adds = chunk_at(index)
        if adds is None:
            raw_copy(index, k).wait_send()
        else:
            pl.when(adds)(sum_of_pair(index, k).wait_send)
            pl.when(jnp.logical_not(adds))(raw_copy(index, k).wait_send)

    @pl.when(root)
    def _():
        for k in range(breadth):
            part_copy(k).wait_send()

    @pl.when(r == 1)
    def _():
        for q in range(1, half):
            stat_copy(q).wait_send()

    pl.when(odd)(chain_copy.wait_send)
    for step in range(1, breadth):
        ps_copy(step)[0].wait_send()
    for step in range(1, height):
        pe_copy(step)[0].wait_send()
    pl.when(jnp.logical_not(itself))(role.wait_send)
    for step in range(2, height, 2):
        wc_copy(r, step, lax.rem(r + step, height)).wait_send()
        wc_copy(lax.rem(r + step, height), step + 1, mate).wait_send()
    wc_copy(r, 1, mate).wait_send()

    @pl.when(has_right)
    def _():
        for k in range(breadth):
            for part in range(2):
                pl.when(k <= c)(right_copy(k, part).wait_send)

    @pl.when(has_left)
    def _():
        for k in range(breadth):
            for part in range(2):
                pl.when(k >= c)(left_copy(k, part).wait_send)


def front(matrix, height, breadth):
    rows, cols = matrix.shape
    width = cols // height
    vmem = pl.BlockSpec(memory_space=pltpu.VMEM)
    dma = pltpu.SemaphoreType.DMA
    scratch = [
        pltpu.VMEM((B, cols), f32),
        pltpu.VMEM((rows, 2 * B), f32),
        pltpu.VMEM((height, B, width), f32),
        pltpu.VMEM((2 * B, cols), bf16),
        pltpu.VMEM((B, 2 * B), f32),
        pltpu.VMEM((breadth, B, 2 * B), f32),
        pltpu.VMEM((B, 2 * B), f32),
        pltpu.VMEM((B, 2 * B), f32),
        pltpu.VMEM((breadth, B, width), f32),
        pltpu.VMEM((breadth, B, width), f32),
        pltpu.VMEM((breadth // 2, B, width), f32),
        pltpu.VMEM((height, B, width), f32),
        pltpu.VMEM((height, B, 2 * B), f32),
        pltpu.VMEM((breadth, B, 2 * B), f32),
        dma((2,)),
        dma((breadth,)),
        dma((height, 2)),
        dma((height, 2)),
        dma((height, 2)),
        dma((breadth,)),
        dma((breadth,)),
        dma((breadth,)),
        dma((breadth,)),
        dma((height // 2,)),
        dma(()),
        dma(()),
        dma(()),
        dma((breadth,)),
        dma((breadth,)),
        dma((breadth,)),
        dma((breadth // 2,)),
        dma((breadth, 2)),
        dma((breadth, 2)),
        dma((breadth, 2)),
        dma(()),
        dma((height,)),
        dma((height,)),
        dma((height,)),
        dma((height,)),
        dma((breadth,)),
        dma((breadth,)),
    ]
    return pl.pallas_call(
        lambda *refs: front_kernel(height, breadth, *refs),
        out_shape=[
            pltpu.VMEM((rows, cols), f32),
            pltpu.VMEM((6 * B, cols), bf16),
            pltpu.VMEM((breadth, B, width), f32),
            pltpu.VMEM((breadth, B, width), f32),
            pltpu.VMEM((B, 6 * B), bf16),
        ],
        in_specs=[pl.BlockSpec(memory_space=pl.ANY)],
        out_specs=[vmem] * 5,
        scratch_shapes=scratch,
        compiler_params=pltpu.CompilerParams(
            collective_id=0, has_side_effects=True, vmem_limit_bytes=20 << 20
        ),
        name="front",
    )(matrix)


def final_kernel(tile, slots, block, right, vr, wr, mix, out, buffer, sems, first_sems):
    rows, cols = block.shape
    width = vr.shape[2]
    size = min(512, cols)
    count = rows // tile

    def copy(i):
        return pltpu.make_async_copy(
            buffer.at[i % slots], out.at[pl.ds(i * tile, tile)], sems.at[i % slots]
        )

    def first_copy(at):
        part = pl.ds(at, size)
        return pltpu.make_async_copy(
            buffer.at[0, :, part], out.at[pl.ds(0, tile), part], first_sems.at[at // size]
        )

    def done(i):
        if i:
            copy(i).wait()
        else:
            for at in range(0, cols, size):
                first_copy(at).wait()

    for i in range(count):
        if i >= slots:
            done(i - slots)
        k, at = i * tile // width, i * tile % width
        v = vr[k, :, at : at + tile]
        u = product_halves(mix[...], jnp.concatenate([wr[k, :, at : at + tile], v], axis=0))
        upper, lower = split(jnp.concatenate([v, u], axis=0).T)
        left = jnp.concatenate([upper, lower, upper], axis=1)
        some = slice(i * tile, (i + 1) * tile)
        for at in range(0, cols, size):
            part = slice(at, at + size)
            buffer[i % slots, :, part] = block[some, part] - jnp.dot(
                left, right[:, part], preferred_element_type=f32
            )
            if not i:
                first_copy(at).start()
        if i:
            copy(i).start()
    for i in range(max(0, count - slots), count):
        done(i)


def final(block, right, vr, wr, mix):
    rows, cols = block.shape
    tile = min(256, vr.shape[2])
    slots = min(4, rows // tile)
    vmem = pl.BlockSpec(memory_space=pltpu.VMEM)
    held = [pltpu.with_memory_space_constraint(x, pltpu.VMEM) for x in (block, right, vr, wr, mix)]
    return pl.pallas_call(
        lambda *refs: final_kernel(tile, slots, *refs),
        out_shape=jax.ShapeDtypeStruct((rows, cols), f32),
        in_specs=[vmem] * 5,
        out_specs=pl.BlockSpec(memory_space=pl.ANY),
        scratch_shapes=[
            pltpu.VMEM((slots, tile, cols), f32),
            pltpu.SemaphoreType.DMA((slots,)),
            pltpu.SemaphoreType.DMA((cols // min(512, cols),)),
        ],
        compiler_params=pltpu.CompilerParams(vmem_limit_bytes=20 << 20),
        name="final",
    )(*held)


def solution(mesh):
    height, breadth = mesh.shape["row"], mesh.shape["col"]

    def shards(matrix):
        return final(*front(matrix, height, breadth))

    return jax.shard_map(
        shards,
        mesh=mesh,
        in_specs=(P("row", "col"),),
        out_specs=P("row", "col"),
        check_vma=False,
    )
```

```python
import jax
import jax.numpy as jnp
from jax import lax
from jax.experimental import pallas as pl
from jax.experimental.pallas import tpu as pltpu
from jax.sharding import PartitionSpec as P

B = 64
STEP = 8
PIECES = 4


highest = lax.Precision.HIGHEST
MESH = pl.DeviceIdType.MESH
f32 = jnp.float32
bf16 = jnp.bfloat16
NT = (((1,), (1,)), ((), ()))
TN = (((0,), (0,)), ((), ()))


def product(left, right):
    return jnp.dot(left, right, precision=highest, preferred_element_type=f32)


def product_nt(left, right):
    return lax.dot_general(left, right, NT, precision=highest, preferred_element_type=f32)


def product_tn(left, right):
    return lax.dot_general(left, right, TN, precision=highest, preferred_element_type=f32)


def split(x):
    upper = x.astype(bf16)
    return upper, (x - upper.astype(f32)).astype(bf16)


def product_halves(left, right):
    upper, lower = split(right)
    return jnp.dot(left, jnp.concatenate([upper, upper, lower], axis=0), preferred_element_type=f32)


def eliminate(work, rows):
    for j in range(0, B, STEP):
        columns = [jnp.broadcast_to(work[:, j + k : j + k + 1], work.shape) for k in range(STEP)]
        lines = [work[j + k : j + k + 1, :] for k in range(STEP)]
        small = [[columns[c][j + r : j + r + 1, :] for c in range(STEP)] for r in range(STEP)]
        scaled = []
        for k in range(STEP):
            inverse = 1.0 / small[k][k]
            scaled.append(lines[k] * inverse)
            for m in range(k + 1, STEP):
                ratio = small[k][m] * inverse
                columns[m] = columns[m] - columns[k] * ratio
                lines[m] = lines[m] - lines[k] * ratio
                for c in range(m, STEP):
                    small[m][c] = small[m][c] - ratio * small[k][c]
        lowered = work
        for k in range(STEP):
            lowered = lowered - columns[k] * scaled[k]
        lowered = jnp.where(rows >= j + STEP, lowered, work)
        for k in range(1, STEP):
            lowered = jnp.where(rows == j + k, lines[k], lowered)
        work = lowered
    return work


def sign_inverse(q, rows):
    lane = lax.broadcasted_iota(jnp.int32, (1, 2 * B), 1)
    signs = jnp.zeros((B, 2 * B), f32)
    for j in range(0, B, STEP):
        columns = [jnp.broadcast_to(q[:, j + k : j + k + 1], q.shape) for k in range(STEP)]
        lines = [q[j + k : j + k + 1, :] for k in range(STEP)]
        small = [[columns[c][j + r : j + r + 1, :] for c in range(STEP)] for r in range(STEP)]
        scaled = []
        chosen = []
        for k in range(STEP):
            sign = jnp.where(small[k][k] >= 0, f32(-1.0), f32(1.0))
            pivot = small[k][k] - sign
            inverse = 1.0 / pivot
            chosen.append(sign)
            lines[k] = jnp.where(lane == j + k, pivot, lines[k]) * inverse
            scaled.append(lines[k])
            for c in range(k + 1, STEP):
                small[k][c] = small[k][c] * inverse
                columns[c] = columns[c] - columns[k] * small[k][c]
            for r in range(STEP):
                if r != k:
                    lines[r] = lines[r] - small[r][k] * lines[k]
                    for c in range(k + 1, STEP):
                        small[r][c] = small[r][c] - small[r][k] * small[k][c]
        for k in range(STEP):
            q = q - columns[k] * scaled[k]
        for k in range(STEP):
            q = jnp.where(rows == j + k, lines[k], q)
            signs = jnp.where(rows == j + k, chosen[k], signs)
    return q[:, B:], signs[:, :1]


def factor_values(gram, top):
    rows = lax.broadcasted_iota(jnp.int32, (B, 2 * B), 0)
    lanes = lax.broadcasted_iota(jnp.int32, (B, 2 * B), 1)
    small_rows = lax.broadcasted_iota(jnp.int32, (B, B), 0)
    small_lanes = lax.broadcasted_iota(jnp.int32, (B, B), 1)
    eye = jnp.where(small_rows == small_lanes, f32(1.0), f32(0.0))
    work = eliminate(jnp.concatenate([gram, eye], axis=1), rows)
    pivots = jnp.sum(jnp.where(rows == lanes, work, f32(0.0)), axis=1, keepdims=True)
    work = work * (1.0 / jnp.sqrt(pivots))
    upper = jnp.where(small_lanes >= small_rows, work[:, :B], f32(0.0))
    lower_inverse = work[:, B:]
    basis = product_nt(top, lower_inverse)
    inverse, signs = sign_inverse(jnp.concatenate([basis, eye], axis=1), rows)
    factor = -product_tn(lower_inverse, product(signs * inverse.T, lower_inverse))
    return factor, (signs * upper).T


def remote(src, dst, send_sem, recv_sem, device):
    return pltpu.make_async_remote_copy(
        src_ref=src,
        dst_ref=dst,
        send_sem=send_sem,
        recv_sem=recv_sem,
        device_id=device,
        device_id_type=MESH,
    )


def front_kernel(
    height, breadth, matrix, block, left, right,
    slab, strip, pc, pr, wr, halves, own, parts, stats, chained, zs, near, rs, wc, pe, ps,
    local_sems, block_sems, pc_recvs, ring_far, ring_sends, mate_send, pr_recvs, pr_sends, part_sends, part_recvs,
    stat_sends, stat_recv, chain_send, chain_recv, raw_sends, near_recvs, rs_sends, rs_recvs, wr_right, wr_left, wr_recvs,
    role_send, wc_recvs, wc_sends, pe_sends, pe_recvs, pt_sends, pt_recvs,
):
    r, c = lax.axis_index("row"), lax.axis_index("col")
    rows, cols = matrix.shape
    width = cols // height
    half = height // 2
    count = height * breadth
    me = r * breadth + c
    core = lax.rem(r, 2)
    chip = r // 2
    even = core == 0
    odd = core == 1
    mate = r + 1 - 2 * core
    place = 2 * (chip // 2) + lax.rem(lax.rem(chip, 2) + chip // 2, 2)

    def seat(q):
        return 2 * (2 * (q // 2) + lax.rem(q + q // 2, 2))

    root = r == 0
    edge = c == 0
    home = r // (height // breadth)
    low_home = home == 0
    high_home = home == breadth - 1
    at_home = jnp.logical_and(high_home, c == breadth - 1)
    reach = jnp.where(high_home, breadth - 2, breadth - 1)

    slab_copy = pltpu.make_async_copy(matrix.at[pl.ds(0, B)], slab, local_sems.at[0])
    strip_copy = pltpu.make_async_copy(matrix.at[:, pl.ds(0, 2 * B)], strip, local_sems.at[1])
    pl.when(root)(slab_copy.start)
    pl.when(edge)(strip_copy.start)
    block_copies = []
    for k in range(breadth):
        part = pl.ds(k * width, width)
        block_copies.append(pltpu.make_async_copy(matrix.at[part], block.at[part], block_sems.at[k]))

    barrier = pltpu.get_barrier_semaphore()

    def greet(step, carry):
        other = lax.rem(me + step, count)
        pl.semaphore_signal(
            barrier, inc=1, device_id=(other // breadth, lax.rem(other, breadth)), device_id_type=MESH
        )
        return carry

    lax.fori_loop(1, count, greet, 0)

    def masked_slab():
        lane = lax.broadcasted_iota(jnp.int32, (B, cols), 1) + c * cols
        return jnp.where(lane >= B, slab[...], f32(0.0))

    @pl.when(root)
    def _():
        slab_copy.wait()
        panel = masked_slab()
        for i in range(height):
            pc[i] = panel[:, i * width : (i + 1) * width]

    pl.when(edge)(strip_copy.wait)
    for copy in block_copies:
        copy.start()

    @pl.when(root)
    def _():
        panel = masked_slab()
        top = jnp.where(edge, slab[:, B : 2 * B], f32(0.0))
        own[...] = jnp.concatenate([product_nt(panel, panel), top], axis=1)

    @pl.when(edge)
    def _():
        for k in range(breadth):
            piece = strip[k * width : (k + 1) * width, :].T[:B, :]
            lane = lax.broadcasted_iota(jnp.int32, (B, width), 1) + r * rows + k * width
            pr[k] = jnp.where(lane >= B, piece, f32(0.0))

    pl.semaphore_wait(barrier, count - 1)

    def piece_copy(i, part, send, target):
        some = pc.at[i, pl.ds(part * (B // PIECES), B // PIECES)]
        return remote(some, some, send, pc_recvs.at[i, part], (target, c))

    def ring_copy(i, part, target):
        return piece_copy(i, part, ring_sends.at[i], target)

    def mate_copy(i, part):
        return piece_copy(i, part, mate_send, mate)

    def chunk_sent(i, send):
        remote(pc.at[i], pc.at[i], send, pc_recvs.at[i, 0], (mate, c)).wait_send()

    def all_sent(send):
        remote(pc, pc, send, pc_recvs.at[0, 0], (mate, c)).wait_send()

    def part_copy(k):
        return remote(own, parts.at[c], part_sends.at[k], part_recvs.at[c], (1, k))

    forth = seat(lax.rem(place + 1, half))
    back = seat(lax.rem(place + half - 1, half))
    straight = half > 2

    def goes(i):
        short = 1 if straight and i % half == half - 1 else 0
        return place + 1 < half - short if i < half else place > 1 + short

    def straight_copy(i, part):
        return piece_copy(i, part, ring_far.at[i // half], back if i < half else forth)

    def ring_on(i, part):
        pl.when(goes(i))(ring_copy(i, part, forth if i < half else back).start)

    def passed(i, part):
        mate_copy(i, part).wait_recv()
        ring_on(i, part)
        mate_copy(i, part).start()

    @pl.when(root)
    def _():
        for k in range(breadth):
            part_copy(k).start()
        for i in range(half):
            for part in range(PIECES):
                ring_copy(i, part, forth).start()
                ring_copy(half + i, part, back).start()
        for part in range(PIECES if straight else 0):
            straight_copy(half - 1, part).start()
            straight_copy(height - 1, part).start()

    def line_copy(k):
        return remote(pr.at[k], pr.at[k], pr_sends.at[k], pr_recvs.at[k], (r, c + 1))

    def line_received(k):
        remote(pr.at[k], pr.at[k], pr_sends.at[k], pr_recvs.at[k], (r, 0)).wait_recv()

    @pl.when(edge)
    def _():
        for k in range(breadth - 1, -1, -1):
            line_copy(k).start()

    middle = jnp.logical_and(c >= 1, c < reach)

    def line_pass(who, index, when=True):
        k = breadth - 1 - index

        @pl.when(jnp.logical_and(jnp.logical_and(middle, c == who), when))
        def _():
            line_received(k)
            line_copy(k).start()

    relays = jnp.logical_and(even, jnp.logical_not(root))

    def halve(i):
        some = slice(i * width, (i + 1) * width)
        upper, lower = split(pc[i])
        halves[:B, some] = upper
        halves[B:, some] = lower

    def go_round(pieces):
        for step, (i, part) in enumerate(pieces):
            passed(i, part)
            if part == PIECES - 1:
                halve(i)
            for index in range(breadth):
                if (index + 1) * len(pieces) // breadth - 1 == step:
                    line_pass(1, index)

    pieces = [(i, part) for i in range(height) for part in range(PIECES)]
    turn = len(pieces) // 2
    later = pieces[turn:] + pieces[:turn]

    @pl.when(jnp.logical_and(relays, 2 * place < half))
    def _():
        go_round(pieces)

    @pl.when(jnp.logical_and(relays, 2 * place == half))
    def _():
        go_round([piece for pair in zip(pieces[:turn], later[:turn]) for piece in pair])

    @pl.when(jnp.logical_and(relays, 2 * place > half))
    def _():
        go_round(later)

    @pl.when(root)
    def _():
        for i in range(height):
            chunk_sent(i, ring_sends.at[i])
        if straight:
            chunk_sent(half - 1, ring_far.at[0])
            chunk_sent(height - 1, ring_far.at[1])
        for i, part in pieces:
            mate_copy(i, part).start()
        for i in range(height):
            halve(i)
        for index in range(breadth):
            line_pass(1, index)

    def stat_copy(q):
        return remote(stats, stats, stat_sends.at[q], stat_recv, (2 * q + 1, c))

    chain_copy = remote(chained, chained, chain_send, chain_recv, (mate, c))

    @pl.when(r == 1)
    def _():
        total = None
        for k in range(breadth):
            remote(parts.at[k], parts.at[k], part_sends.at[k], part_recvs.at[k], (0, c)).wait_recv()
            total = parts[k] if total is None else total + parts[k]
        stats[...] = total
        for q in range(1, half):
            stat_copy(q).start()

    pl.when(odd)(lambda: line_pass(1, 0))

    @pl.when(jnp.logical_and(odd, r != 1))
    def _():
        remote(stats, stats, stat_sends.at[0], stat_recv, (1, c)).wait_recv()

    @pl.when(odd)
    def _():
        factor, turned = factor_values(stats[:, :B], stats[:, B:].T)
        chained[...] = jnp.concatenate([factor, turned], axis=1)
        chain_copy.start()
        for index in range(1, breadth):
            line_pass(1, index)
        for i, part in pieces:
            mate_copy(i, part).wait_recv()
            if part == PIECES - 1:
                halve(i)

    @pl.when(even)
    def _():
        all_sent(mate_send)
        chain_copy.wait_recv()

    @pl.when(relays)
    def _():
        for i in range(height):
            pl.when(goes(i))(lambda: chunk_sent(i, ring_sends.at[i]))

    def lower_top(buffer):
        for i in range(buffer.shape[0]):
            low, high = max(B, i * width), min(2 * B, (i + 1) * width)
            if low < high:
                lanes = slice(low - i * width, high - i * width)
                buffer[i, :, lanes] = buffer[i, :, lanes] - chained[:, low : high]

    @pl.when(edge)
    def _():
        lower_top(pc)
        for i in range(height):
            if max(B, i * width) < min(2 * B, (i + 1) * width):
                halve(i)

    @pl.when(at_home)
    def _():
        for k in range(breadth):
            pr[k] = pc[lax.rem(r * breadth + k, height)]

    for copy in block_copies:
        copy.wait()

    size = min(512, cols)

    pair = c // 2
    late = lax.rem(c, 2)
    friend = c + 1 - 2 * late
    pairs = breadth // 2

    def raw_copy(index, k):
        return remote(zs.at[k], near.at[k], raw_sends.at[index], near_recvs.at[k], (r, friend))

    def sum_of_pair(index, k):
        return remote(zs.at[k], rs.at[pair], rs_sends.at[index], rs_recvs.at[pair], (r, k))

    def chunk_at(index):
        if index < breadth - 2:
            whose = lax.rem(pair + 1 + index // 2, pairs)
            above = jnp.where(whose > pair, 1, 0)
            first = jnp.where(whose > pair, 1 - index % 2, index % 2)
            return 2 * whose + first, above == late
        return (friend if index == breadth - 2 else c), None

    def add_pair(index):
        k, adds = chunk_at(index)

        @pl.when(adds)
        def _():
            raw_copy(index, k).wait_recv()
            zs[k] = zs[k] + near[k]
            sum_of_pair(index, k).start()

    for index in range(breadth):
        if index in (0, breadth // 2):
            for k in range(breadth // 2):
                line_pass(2, k, (r >= 2) if index == 0 else (r < 2))
        other, adds = chunk_at(index)
        some = pl.ds(pl.multiple_of(other * width, width), width)
        both = jnp.zeros((width, 2 * B), f32)
        for start in range(0, cols, size):
            part = slice(start, start + size)
            upper, lower = split(block[some, part])
            both = both + lax.dot_general(upper, halves[:, part], NT, preferred_element_type=f32)
            low = lax.dot_general(lower, halves[:, part], NT, preferred_element_type=f32)
            both = both + jnp.where(lax.broadcasted_iota(jnp.int32, both.shape, 1) < B, low, f32(0.0))
        turned = both.T
        value = turned[:B, :] + turned[B:, :]
        zs[other] = value
        if index < breadth - 2:
            pl.when(jnp.logical_not(adds))(raw_copy(index, other).start)
        elif index == breadth - 2:
            raw_copy(index, other).start()
        if index >= 2:
            add_pair(index - 2)
    for k in range(breadth // 2, breadth):
        line_pass(2, k)
    for who in range(3, breadth - 1):
        for k in range(breadth):
            line_pass(who, k)

    raw_copy(0, c).wait_recv()
    total = zs[c] + near[c]
    for step in range(1, pairs):
        other = lax.rem(pair + step, pairs)
        remote(rs.at[other], rs.at[other], rs_sends.at[0], rs_recvs.at[other], (r, friend)).wait_recv()
        total = total + rs[other]
    wr[c] = total

    def sum_copy(k, part, sends, target):
        some = wr.at[k, pl.ds(part * (B // 2), B // 2)]
        return remote(some, some, sends.at[k, part], wr_recvs.at[k, part], (r, target))

    def right_copy(k, part):
        return sum_copy(k, part, wr_right, c + 1)

    def left_copy(k, part):
        return sum_copy(k, part, wr_left, c - 1)

    has_right = jnp.logical_and(c + 1 < breadth, jnp.logical_not(jnp.logical_and(high_home, c == breadth - 2)))
    has_left = jnp.logical_and(c >= 1, jnp.logical_not(jnp.logical_and(low_home, c == 1)))
    takes_right = jnp.logical_not(jnp.logical_and(low_home, edge))
    takes_left = jnp.logical_not(jnp.logical_and(high_home, c == breadth - 1))
    to_row = lax.rem(me, height)
    to_col = me // height
    itself = jnp.logical_and(to_row == r, to_col == c)
    role = remote(wr.at[c], wc.at[to_row], role_send, wc_recvs.at[to_row], (to_row, to_col))
    pl.when(jnp.logical_not(itself))(role.start)
    for part in range(2):
        pl.when(has_right)(right_copy(c, part).start)
        pl.when(has_left)(left_copy(c, part).start)

    @pl.when(itself)
    def _():
        wc[r] = total

    @pl.when(c == reach)
    def _():
        line_received(c)

    slots = lax.broadcasted_iota(jnp.int32, (B, width), 0)
    positions = lax.broadcasted_iota(jnp.int32, (B, width), 1) + me * width - B
    onehot = jnp.where(positions == slots, f32(1.0), f32(0.0))
    vector = pr[c] - product(chained[:, B:], onehot)
    pe[r] = jnp.concatenate([product_nt(total, vector), jnp.zeros((B, B), f32)], axis=1)

    def pe_copy(step):
        other = lax.rem(r + step, height)
        return remote(pe.at[r], pe.at[r], pe_sends.at[step], pe_recvs.at[r], (other, c)), other

    for step in range(1, height):
        pe_copy(step)[0].start()

    def wr_pass(s):
        for part in range(2):

            @pl.when(jnp.logical_and(c - s >= 0, takes_left))
            def _():
                sum_copy(c - s, part, wr_right, c - 1).wait_recv()
                pl.when(has_right)(right_copy(c - s, part).start)

            @pl.when(jnp.logical_and(c + s < breadth, takes_right))
            def _():
                sum_copy(c + s, part, wr_left, c + 1).wait_recv()
                pl.when(has_left)(left_copy(c + s, part).start)

    def wc_copy(slot, step, other):
        return remote(wc.at[slot], wc.at[slot], wc_sends.at[step], wc_recvs.at[slot], (other, c))

    def wc_received(slot):
        remote(wc.at[slot], wc.at[slot], wc_sends.at[0], wc_recvs.at[slot], (mate, c)).wait_recv()

    pl.when(jnp.logical_not(itself))(lambda: wc_received(r))
    for step in range(2, height, 2):
        wc_copy(r, step, lax.rem(r + step, height)).start()
    wc_copy(r, 1, mate).start()
    wr_pass(1)
    summed = pe[r]
    for step in range(1, height):
        copy, other = pe_copy(step)
        remote(pe.at[other], pe.at[other], pe_sends.at[step], pe_recvs.at[other], (other, c)).wait_recv()
        summed = summed + pe[other]
    ps[c] = summed

    def ps_copy(step):
        other = lax.rem(c + step, breadth)
        return remote(ps.at[c], ps.at[c], pt_sends.at[step], pt_recvs.at[c], (r, other)), other

    for step in range(1, breadth):
        ps_copy(step)[0].start()
    for s in range(2, breadth - 1):
        wr_pass(s)
    for step in range(2, height, 2):
        slot = lax.rem(r + step, height)
        wc_received(slot)
        wc_copy(slot, step + 1, mate).start()
    if breadth > 2:
        wr_pass(breadth - 1)
    projected = ps[c]
    for step in range(1, breadth):
        copy, other = ps_copy(step)
        remote(ps.at[other], ps.at[other], pt_sends.at[step], pt_recvs.at[other], (r, other)).wait_recv()
        projected = projected + ps[other]

    factor = chained[:, :B]
    turned = factor.T
    inner = product(turned, product(projected[:, :B], factor))
    upper, lower = split(jnp.concatenate([turned, -0.5 * inner], axis=1))
    mix = jnp.concatenate([upper, lower, upper], axis=1)
    wc_received(mate)
    for step in range(2, height, 2):
        wc_received(lax.rem(mate + step, height))
    for i in range(height):
        part = slice(i * width, (i + 1) * width)
        v = pc[i]
        u = product_halves(mix, jnp.concatenate([wc[i], v], axis=0))
        upper, lower = split(jnp.concatenate([u, v], axis=0))
        right[: 2 * B, part] = upper
        right[2 * B : 4 * B, part] = upper
        right[4 * B :, part] = lower

    @pl.when(c == reach)
    def _():
        for k in range(breadth):
            pl.when(k != c)(lambda: line_received(k))

    @pl.when(c < reach)
    def _():
        for k in range(breadth):
            line_copy(k).wait_send()

    @pl.when(root)
    def _():
        lower_top(pr)

    @pl.when(jnp.logical_not(jnp.logical_and(takes_left, takes_right)))
    def _():
        for k in range(breadth):

            @pl.when(k != c)
            def _():
                wr[k] = wc[lax.rem(r * breadth + k, height)]

    for i in range(breadth):
        part = slice(i * width, (i + 1) * width)
        v = pr[i]
        u = product_halves(mix, jnp.concatenate([wr[i], v], axis=0))
        upper, lower = split(jnp.concatenate([v, u], axis=0).T)
        left[part, : 2 * B] = upper
        left[part, 2 * B : 4 * B] = lower
        left[part, 4 * B :] = upper
    for index in range(breadth - 1):
        k, adds = chunk_at(index)
        if adds is None:
            raw_copy(index, k).wait_send()
        else:
            pl.when(adds)(sum_of_pair(index, k).wait_send)
            pl.when(jnp.logical_not(adds))(raw_copy(index, k).wait_send)

    @pl.when(root)
    def _():
        for k in range(breadth):
            part_copy(k).wait_send()

    @pl.when(r == 1)
    def _():
        for q in range(1, half):
            stat_copy(q).wait_send()

    pl.when(odd)(chain_copy.wait_send)
    for step in range(1, breadth):
        ps_copy(step)[0].wait_send()
    for step in range(1, height):
        pe_copy(step)[0].wait_send()
    pl.when(jnp.logical_not(itself))(role.wait_send)
    for step in range(2, height, 2):
        wc_copy(r, step, lax.rem(r + step, height)).wait_send()
        wc_copy(lax.rem(r + step, height), step + 1, mate).wait_send()
    wc_copy(r, 1, mate).wait_send()

    @pl.when(has_right)
    def _():
        for k in range(breadth):
            for part in range(2):
                pl.when(k <= c)(right_copy(k, part).wait_send)

    @pl.when(has_left)
    def _():
        for k in range(breadth):
            for part in range(2):
                pl.when(k >= c)(left_copy(k, part).wait_send)


def front(matrix, height, breadth):
    rows, cols = matrix.shape
    width = cols // height
    vmem = pl.BlockSpec(memory_space=pltpu.VMEM)
    dma = pltpu.SemaphoreType.DMA
    scratch = [
        pltpu.VMEM((B, cols), f32),
        pltpu.VMEM((rows, 2 * B), f32),
        pltpu.VMEM((height, B, width), f32),
        pltpu.VMEM((breadth, B, width), f32),
        pltpu.VMEM((breadth, B, width), f32),
        pltpu.VMEM((2 * B, cols), bf16),
        pltpu.VMEM((B, 2 * B), f32),
        pltpu.VMEM((breadth, B, 2 * B), f32),
        pltpu.VMEM((B, 2 * B), f32),
        pltpu.VMEM((B, 2 * B), f32),
        pltpu.VMEM((breadth, B, width), f32),
        pltpu.VMEM((breadth, B, width), f32),
        pltpu.VMEM((breadth // 2, B, width), f32),
        pltpu.VMEM((height, B, width), f32),
        pltpu.VMEM((height, B, 2 * B), f32),
        pltpu.VMEM((breadth, B, 2 * B), f32),
        dma((2,)),
        dma((breadth,)),
        dma((height, PIECES)),
        dma((2,)),
        dma((height,)),
        dma(()),
        dma((breadth,)),
        dma((breadth,)),
        dma((breadth,)),
        dma((breadth,)),
        dma((height // 2,)),
        dma(()),
        dma(()),
        dma(()),
        dma((breadth,)),
        dma((breadth,)),
        dma((breadth,)),
        dma((breadth // 2,)),
        dma((breadth, 2)),
        dma((breadth, 2)),
        dma((breadth, 2)),
        dma(()),
        dma((height,)),
        dma((height,)),
        dma((height,)),
        dma((height,)),
        dma((breadth,)),
        dma((breadth,)),
    ]
    return pl.pallas_call(
        lambda *refs: front_kernel(height, breadth, *refs),
        out_shape=[
            pltpu.VMEM((rows, cols), f32),
            pltpu.VMEM((rows, 6 * B), bf16),
            pltpu.VMEM((6 * B, cols), bf16),
        ],
        in_specs=[pl.BlockSpec(memory_space=pl.ANY)],
        out_specs=[vmem] * 3,
        scratch_shapes=scratch,
        compiler_params=pltpu.CompilerParams(
            collective_id=0, has_side_effects=True, vmem_limit_bytes=20 << 20
        ),
        name="front",
    )(matrix)


def final_kernel(tile, slots, block, left, right, out, buffer, sems, first_sems):
    rows, cols = block.shape
    size = min(512, cols)
    count = rows // tile

    def copy(i):
        return pltpu.make_async_copy(
            buffer.at[i % slots], out.at[pl.ds(i * tile, tile)], sems.at[i % slots]
        )

    def first_copy(at):
        part = pl.ds(at, size)
        return pltpu.make_async_copy(
            buffer.at[0, :, part], out.at[pl.ds(0, tile), part], first_sems.at[at // size]
        )

    def done(i):
        if i:
            copy(i).wait()
        else:
            for at in range(0, cols, size):
                first_copy(at).wait()

    for i in range(count):
        if i >= slots:
            done(i - slots)
        some = slice(i * tile, (i + 1) * tile)
        for at in range(0, cols, size):
            part = slice(at, at + size)
            buffer[i % slots, :, part] = block[some, part] - jnp.dot(
                left[some, :], right[:, part], preferred_element_type=f32
            )
            if not i:
                first_copy(at).start()
        if i:
            copy(i).start()
    for i in range(max(0, count - slots), count):
        done(i)


def final(block, left, right):
    rows, cols = block.shape
    tile = min(256, rows)
    slots = min(4, rows // tile)
    vmem = pl.BlockSpec(memory_space=pltpu.VMEM)
    held = [pltpu.with_memory_space_constraint(x, pltpu.VMEM) for x in (block, left, right)]
    return pl.pallas_call(
        lambda *refs: final_kernel(tile, slots, *refs),
        out_shape=jax.ShapeDtypeStruct((rows, cols), f32),
        in_specs=[vmem] * 3,
        out_specs=pl.BlockSpec(memory_space=pl.ANY),
        scratch_shapes=[
            pltpu.VMEM((slots, tile, cols), f32),
            pltpu.SemaphoreType.DMA((slots,)),
            pltpu.SemaphoreType.DMA((cols // min(512, cols),)),
        ],
        compiler_params=pltpu.CompilerParams(vmem_limit_bytes=20 << 20),
        name="final",
    )(*held)


def solution(mesh):
    height, breadth = mesh.shape["row"], mesh.shape["col"]

    def shards(matrix):
        return final(*front(matrix, height, breadth))

    return jax.shard_map(
        shards,
        mesh=mesh,
        in_specs=(P("row", "col"),),
        out_specs=P("row", "col"),
        check_vma=False,
    )
```

```python
import jax
import jax.numpy as jnp
from jax import lax
from jax.experimental import pallas as pl
from jax.experimental.pallas import tpu as pltpu
from jax.sharding import PartitionSpec as P

B = 64
STEP = 8
PIECES = 4


highest = lax.Precision.HIGHEST
MESH = pl.DeviceIdType.MESH
f32 = jnp.float32
bf16 = jnp.bfloat16
NT = (((1,), (1,)), ((), ()))
TN = (((0,), (0,)), ((), ()))


def product(left, right):
    return jnp.dot(left, right, precision=highest, preferred_element_type=f32)


def product_nt(left, right):
    return lax.dot_general(left, right, NT, precision=highest, preferred_element_type=f32)


def product_tn(left, right):
    return lax.dot_general(left, right, TN, precision=highest, preferred_element_type=f32)


def split(x):
    upper = x.astype(bf16)
    return upper, (x - upper.astype(f32)).astype(bf16)


def product_halves(left, right):
    upper, lower = split(right)
    return jnp.dot(left, jnp.concatenate([upper, upper, lower], axis=0), preferred_element_type=f32)


def eliminate(work, rows):
    for j in range(0, B, STEP):
        columns = [jnp.broadcast_to(work[:, j + k : j + k + 1], work.shape) for k in range(STEP)]
        lines = [work[j + k : j + k + 1, :] for k in range(STEP)]
        small = [[columns[c][j + r : j + r + 1, :] for c in range(STEP)] for r in range(STEP)]
        scaled = []
        for k in range(STEP):
            inverse = 1.0 / small[k][k]
            scaled.append(lines[k] * inverse)
            for m in range(k + 1, STEP):
                ratio = small[k][m] * inverse
                columns[m] = columns[m] - columns[k] * ratio
                lines[m] = lines[m] - lines[k] * ratio
                for c in range(m, STEP):
                    small[m][c] = small[m][c] - ratio * small[k][c]
        lowered = work
        for k in range(STEP):
            lowered = lowered - columns[k] * scaled[k]
        lowered = jnp.where(rows >= j + STEP, lowered, work)
        for k in range(1, STEP):
            lowered = jnp.where(rows == j + k, lines[k], lowered)
        work = lowered
    return work


def sign_inverse(q, rows):
    lane = lax.broadcasted_iota(jnp.int32, (1, 2 * B), 1)
    signs = jnp.zeros((B, 2 * B), f32)
    for j in range(0, B, STEP):
        columns = [jnp.broadcast_to(q[:, j + k : j + k + 1], q.shape) for k in range(STEP)]
        lines = [q[j + k : j + k + 1, :] for k in range(STEP)]
        small = [[columns[c][j + r : j + r + 1, :] for c in range(STEP)] for r in range(STEP)]
        scaled = []
        chosen = []
        for k in range(STEP):
            sign = jnp.where(small[k][k] >= 0, f32(-1.0), f32(1.0))
            pivot = small[k][k] - sign
            inverse = 1.0 / pivot
            chosen.append(sign)
            lines[k] = jnp.where(lane == j + k, pivot, lines[k]) * inverse
            scaled.append(lines[k])
            for c in range(k + 1, STEP):
                small[k][c] = small[k][c] * inverse
                columns[c] = columns[c] - columns[k] * small[k][c]
            for r in range(STEP):
                if r != k:
                    lines[r] = lines[r] - small[r][k] * lines[k]
                    for c in range(k + 1, STEP):
                        small[r][c] = small[r][c] - small[r][k] * small[k][c]
        for k in range(STEP):
            q = q - columns[k] * scaled[k]
        for k in range(STEP):
            q = jnp.where(rows == j + k, lines[k], q)
            signs = jnp.where(rows == j + k, chosen[k], signs)
    return q[:, B:], signs[:, :1]


def factor_values(gram, top):
    rows = lax.broadcasted_iota(jnp.int32, (B, 2 * B), 0)
    lanes = lax.broadcasted_iota(jnp.int32, (B, 2 * B), 1)
    small_rows = lax.broadcasted_iota(jnp.int32, (B, B), 0)
    small_lanes = lax.broadcasted_iota(jnp.int32, (B, B), 1)
    eye = jnp.where(small_rows == small_lanes, f32(1.0), f32(0.0))
    work = eliminate(jnp.concatenate([gram, eye], axis=1), rows)
    pivots = jnp.sum(jnp.where(rows == lanes, work, f32(0.0)), axis=1, keepdims=True)
    work = work * (1.0 / jnp.sqrt(pivots))
    upper = jnp.where(small_lanes >= small_rows, work[:, :B], f32(0.0))
    lower_inverse = work[:, B:]
    basis = product_nt(top, lower_inverse)
    inverse, signs = sign_inverse(jnp.concatenate([basis, eye], axis=1), rows)
    factor = -product_tn(lower_inverse, product(signs * inverse.T, lower_inverse))
    return factor, (signs * upper).T


def remote(src, dst, send_sem, recv_sem, device):
    return pltpu.make_async_remote_copy(
        src_ref=src,
        dst_ref=dst,
        send_sem=send_sem,
        recv_sem=recv_sem,
        device_id=device,
        device_id_type=MESH,
    )


def front_kernel(
    height, breadth, matrix, block, left, right,
    slab, strip, pc, pr, wr, halves, own, parts, stats, chained, zs, near, rs, wc, pe, ps, sums,
    local_sems, block_sems, pc_recvs, ring_far, ring_sends, mate_send, pr_recvs, pr_sends, part_send, part_recvs,
    stat_sends, stat_recv, chain_send, chain_recv, raw_sends, near_recvs, rs_sends, rs_recvs, wr_right, wr_left, wr_recvs,
    role_send, wc_recvs, wc_send, pe_send, pe_recvs, ps_send, pt_recvs,
):
    r, c = lax.axis_index("row"), lax.axis_index("col")
    rows, cols = matrix.shape
    width = cols // height
    half = height // 2
    count = height * breadth
    me = r * breadth + c
    core = lax.rem(r, 2)
    chip = r // 2
    even = core == 0
    odd = core == 1
    mate = r + 1 - 2 * core
    place = 2 * (chip // 2) + lax.rem(lax.rem(chip, 2) + chip // 2, 2)

    def seat(q):
        return 2 * (2 * (q // 2) + lax.rem(q + q // 2, 2))

    root = r == 0
    edge = c == 0
    home = r // (height // breadth)
    low_home = home == 0
    high_home = home == breadth - 1
    at_home = jnp.logical_and(high_home, c == breadth - 1)
    reach = jnp.where(high_home, breadth - 2, breadth - 1)

    pair = c // 2
    late = lax.rem(c, 2)
    friend = c + 1 - 2 * late
    pairs = breadth // 2

    def chunk_at(index):
        if index < breadth - 2:
            whose = lax.rem(pair + 1 + index // 2, pairs)
            above = jnp.where(whose > pair, 1, 0)
            first = jnp.where(whose > pair, 1 - index % 2, index % 2)
            return 2 * whose + first, above == late
        return (friend if index == breadth - 2 else c), None

    slab_copy = pltpu.make_async_copy(matrix.at[pl.ds(0, B)], slab, local_sems.at[0])
    strip_copy = pltpu.make_async_copy(matrix.at[:, pl.ds(0, 2 * B)], strip, local_sems.at[1])
    pl.when(root)(slab_copy.start)
    pl.when(edge)(strip_copy.start)
    def block_rows(index):
        k = chunk_at(index)[0]
        return pl.ds(pl.multiple_of(k * width, width), width)

    def block_copy(index):
        part = block_rows(index)
        return pltpu.make_async_copy(matrix.at[part], block.at[part], block_sems.at[index])

    sums[...] = jnp.zeros_like(sums)
    barrier = pltpu.get_barrier_semaphore()

    def greet(step, carry):
        other = lax.rem(me + step, count)
        pl.semaphore_signal(
            barrier, inc=1, device_id=(other // breadth, lax.rem(other, breadth)), device_id_type=MESH
        )
        return carry

    lax.fori_loop(1, count, greet, 0)

    def masked_slab():
        lane = lax.broadcasted_iota(jnp.int32, (B, cols), 1) + c * cols
        return jnp.where(lane >= B, slab[...], f32(0.0))

    @pl.when(root)
    def _():
        slab_copy.wait()
        panel = masked_slab()
        for i in range(height):
            pc[i] = panel[:, i * width : (i + 1) * width]

    pl.when(edge)(strip_copy.wait)
    for index in range(breadth):
        block_copy(index).start()

    @pl.when(root)
    def _():
        panel = masked_slab()
        top = jnp.where(edge, slab[:, B : 2 * B], f32(0.0))
        own[...] = jnp.concatenate([product_nt(panel, panel), top], axis=1)

    @pl.when(edge)
    def _():
        for k in range(breadth):
            piece = strip[k * width : (k + 1) * width, :].T[:B, :]
            lane = lax.broadcasted_iota(jnp.int32, (B, width), 1) + r * rows + k * width
            pr[k] = jnp.where(lane >= B, piece, f32(0.0))

    pl.semaphore_wait(barrier, count - 1)

    def piece_copy(i, part, send, target):
        some = pc.at[i, pl.ds(part * (B // PIECES), B // PIECES)]
        return remote(some, some, send, pc_recvs.at[i, part], (target, c))

    def ring_copy(i, part, target):
        return piece_copy(i, part, ring_sends.at[i], target)

    def mate_copy(i, part):
        return piece_copy(i, part, mate_send, mate)

    def chunk_sent(i, send):
        remote(pc.at[i], pc.at[i], send, pc_recvs.at[i, 0], (mate, c)).wait_send()

    def all_sent(send):
        remote(pc, pc, send, pc_recvs.at[0, 0], (mate, c)).wait_send()

    def part_copy(k):
        return remote(own, parts.at[c], part_send, part_recvs.at[c], (1, k))

    forth = seat(lax.rem(place + 1, half))
    back = seat(lax.rem(place + half - 1, half))
    straight = half > 2

    def goes(i):
        short = 1 if straight and i % half == half - 1 else 0
        return place + 1 < half - short if i < half else place > 1 + short

    def straight_copy(i, part):
        return piece_copy(i, part, ring_far.at[i // half], back if i < half else forth)

    def ring_on(i, part):
        pl.when(goes(i))(ring_copy(i, part, forth if i < half else back).start)

    def passed(i, part):
        mate_copy(i, part).wait_recv()
        ring_on(i, part)
        mate_copy(i, part).start()

    @pl.when(root)
    def _():
        for k in range(breadth):
            part_copy(k).start()
        for i in range(half):
            for part in range(PIECES):
                ring_copy(i, part, forth).start()
                ring_copy(half + i, part, back).start()
        for part in range(PIECES if straight else 0):
            straight_copy(half - 1, part).start()
            straight_copy(height - 1, part).start()

    def line_copy(k):
        return remote(pr.at[k], pr.at[k], pr_sends.at[k], pr_recvs.at[k], (r, c + 1))

    def line_received(k):
        remote(pr.at[k], pr.at[k], pr_sends.at[k], pr_recvs.at[k], (r, 0)).wait_recv()

    @pl.when(edge)
    def _():
        for k in range(breadth - 1, -1, -1):
            line_copy(k).start()

    middle = jnp.logical_and(c >= 1, c < reach)

    def line_pass(who, index, when=True):
        k = breadth - 1 - index

        @pl.when(jnp.logical_and(jnp.logical_and(middle, c == who), when))
        def _():
            line_received(k)
            line_copy(k).start()

    relays = jnp.logical_and(even, jnp.logical_not(root))

    def share(some, part):
        upper, lower = split(block[some, part])
        both = lax.dot_general(upper, halves[:, part], NT, preferred_element_type=f32)
        low = lax.dot_general(lower, halves[:, part], NT, preferred_element_type=f32)
        return both + jnp.where(lax.broadcasted_iota(jnp.int32, both.shape, 1) < B, low, f32(0.0))

    topmost = [i for i in range(height) if max(B, i * width) < min(2 * B, (i + 1) * width)]

    def halve(i):
        some = slice(i * width, (i + 1) * width)
        upper, lower = split(pc[i])
        halves[:B, some] = upper
        halves[B:, some] = lower
        if i not in topmost:
            sums[...] = sums[...] + share(block_rows(0), some)

    block_copy(0).wait()

    def go_round(pieces):
        for step, (i, part) in enumerate(pieces):
            passed(i, part)
            if part == PIECES - 1:
                halve(i)
            for index in range(breadth):
                if (index + 1) * len(pieces) // breadth - 1 == step:
                    line_pass(1, index)

    pieces = [(i, part) for i in range(height) for part in range(PIECES)]
    turn = len(pieces) // 2
    later = pieces[turn:] + pieces[:turn]

    @pl.when(jnp.logical_and(relays, 2 * place < half))
    def _():
        go_round(pieces)

    @pl.when(jnp.logical_and(relays, 2 * place == half))
    def _():
        go_round([piece for pair in zip(pieces[:turn], later[:turn]) for piece in pair])

    @pl.when(jnp.logical_and(relays, 2 * place > half))
    def _():
        go_round(later)

    @pl.when(root)
    def _():
        for i in range(height):
            chunk_sent(i, ring_sends.at[i])
        if straight:
            chunk_sent(half - 1, ring_far.at[0])
            chunk_sent(height - 1, ring_far.at[1])
        for i, part in pieces:
            mate_copy(i, part).start()
        for i in range(height):
            halve(i)
        for index in range(breadth):
            line_pass(1, index)

    def stat_copy(q):
        return remote(stats, stats, stat_sends.at[q], stat_recv, (2 * q + 1, c))

    chain_copy = remote(chained, chained, chain_send, chain_recv, (mate, c))

    @pl.when(r == 1)
    def _():
        total = None
        for k in range(breadth):
            remote(parts.at[k], parts.at[k], part_send, part_recvs.at[k], (0, c)).wait_recv()
            total = parts[k] if total is None else total + parts[k]
        stats[...] = total
        for q in range(1, half):
            stat_copy(q).start()

    pl.when(odd)(lambda: line_pass(1, 0))

    @pl.when(jnp.logical_and(odd, r != 1))
    def _():
        remote(stats, stats, stat_sends.at[0], stat_recv, (1, c)).wait_recv()

    @pl.when(odd)
    def _():
        factor, turned = factor_values(stats[:, :B], stats[:, B:].T)
        chained[...] = jnp.concatenate([factor, turned], axis=1)
        chain_copy.start()
        for index in range(1, breadth):
            line_pass(1, index)
        for i, part in pieces:
            mate_copy(i, part).wait_recv()
            if part == PIECES - 1:
                halve(i)

    @pl.when(even)
    def _():
        all_sent(mate_send)
        chain_copy.wait_recv()

    @pl.when(relays)
    def _():
        for i in range(height):
            pl.when(goes(i))(lambda: chunk_sent(i, ring_sends.at[i]))

    def lower_top(buffer):
        for i in range(buffer.shape[0]):
            low, high = max(B, i * width), min(2 * B, (i + 1) * width)
            if low < high:
                lanes = slice(low - i * width, high - i * width)
                buffer[i, :, lanes] = buffer[i, :, lanes] - chained[:, low : high]

    @pl.when(edge)
    def _():
        lower_top(pc)
        for i in topmost:
            halve(i)

    @pl.when(at_home)
    def _():
        for k in range(breadth):
            pr[k] = pc[lax.rem(r * breadth + k, height)]

    for index in range(1, breadth):
        block_copy(index).wait()

    size = min(512, cols)

    def raw_copy(index, k):
        return remote(zs.at[k], near.at[k], raw_sends.at[index], near_recvs.at[k], (r, friend))

    def sum_of_pair(index, k):
        return remote(zs.at[k], rs.at[pair], rs_sends.at[index], rs_recvs.at[pair], (r, k))

    def add_pair(index):
        k, adds = chunk_at(index)

        @pl.when(adds)
        def _():
            raw_copy(index, k).wait_recv()
            zs[k] = zs[k] + near[k]
            sum_of_pair(index, k).start()

    for index in range(breadth):
        if index in (0, breadth // 2):
            for k in range(breadth // 2):
                line_pass(2, k, (r >= 2) if index == 0 else (r < 2))
        other, adds = chunk_at(index)
        some = block_rows(index)
        if index == 0:
            both = sums[...]
            for i in topmost:
                both = both + share(some, slice(i * width, (i + 1) * width))
        else:
            both = jnp.zeros((width, 2 * B), f32)
            for start in range(0, cols, size):
                both = both + share(some, slice(start, start + size))
        turned = both.T
        value = turned[:B, :] + turned[B:, :]
        zs[other] = value
        if index < breadth - 2:
            pl.when(jnp.logical_not(adds))(raw_copy(index, other).start)
        elif index == breadth - 2:
            raw_copy(index, other).start()
        if index >= 2:
            add_pair(index - 2)
    for k in range(breadth // 2, breadth):
        line_pass(2, k)
    for who in range(3, breadth - 1):
        for k in range(breadth):
            line_pass(who, k)

    raw_copy(0, c).wait_recv()
    total = zs[c] + near[c]
    for step in range(1, pairs):
        other = lax.rem(pair + step, pairs)
        remote(rs.at[other], rs.at[other], rs_sends.at[0], rs_recvs.at[other], (r, friend)).wait_recv()
        total = total + rs[other]
    wr[c] = total

    def sum_copy(k, part, sends, target):
        some = wr.at[k, pl.ds(part * (B // 2), B // 2)]
        return remote(some, some, sends.at[k], wr_recvs.at[k, part], (r, target))

    def sum_sent(k, sends):
        remote(wr.at[k], wr.at[k], sends.at[k], wr_recvs.at[k, 0], (r, c)).wait_send()

    def right_copy(k, part):
        return sum_copy(k, part, wr_right, c + 1)

    def left_copy(k, part):
        return sum_copy(k, part, wr_left, c - 1)

    has_right = jnp.logical_and(c + 1 < breadth, jnp.logical_not(jnp.logical_and(high_home, c == breadth - 2)))
    has_left = jnp.logical_and(c >= 1, jnp.logical_not(jnp.logical_and(low_home, c == 1)))
    takes_right = jnp.logical_not(jnp.logical_and(low_home, edge))
    takes_left = jnp.logical_not(jnp.logical_and(high_home, c == breadth - 1))
    to_row = lax.rem(me, height)
    to_col = me // height
    itself = jnp.logical_and(to_row == r, to_col == c)
    role = remote(wr.at[c], wc.at[to_row], role_send, wc_recvs.at[to_row], (to_row, to_col))
    pl.when(jnp.logical_not(itself))(role.start)
    for part in range(2):
        pl.when(has_right)(right_copy(c, part).start)
        pl.when(has_left)(left_copy(c, part).start)

    @pl.when(itself)
    def _():
        wc[r] = total

    @pl.when(c == reach)
    def _():
        line_received(c)

    slots = lax.broadcasted_iota(jnp.int32, (B, width), 0)
    positions = lax.broadcasted_iota(jnp.int32, (B, width), 1) + me * width - B
    onehot = jnp.where(positions == slots, f32(1.0), f32(0.0))
    vector = pr[c] - product(chained[:, B:], onehot)
    part_of = product_nt(total, vector)
    pe[r] = jnp.concatenate([part_of[: B // 2], part_of[B // 2 :]], axis=1)

    def pe_copy(step):
        other = lax.rem(r + step, height)
        return remote(pe.at[r], pe.at[r], pe_send, pe_recvs.at[r], (other, c)), other

    for step in range(1, height):
        pe_copy(step)[0].start()

    def wr_pass(s):
        for part in range(2):

            @pl.when(jnp.logical_and(c - s >= 0, takes_left))
            def _():
                sum_copy(c - s, part, wr_right, c - 1).wait_recv()
                pl.when(has_right)(right_copy(c - s, part).start)

            @pl.when(jnp.logical_and(c + s < breadth, takes_right))
            def _():
                sum_copy(c + s, part, wr_left, c + 1).wait_recv()
                pl.when(has_left)(left_copy(c + s, part).start)

    def wc_copy(slot, step, other):
        return remote(wc.at[slot], wc.at[slot], wc_send, wc_recvs.at[slot], (other, c))

    def wc_received(slot):
        remote(wc.at[slot], wc.at[slot], wc_send, wc_recvs.at[slot], (mate, c)).wait_recv()

    pl.when(jnp.logical_not(itself))(lambda: wc_received(r))
    for step in range(2, height, 2):
        wc_copy(r, step, lax.rem(r + step, height)).start()
    wc_copy(r, 1, mate).start()
    wr_pass(1)
    summed = pe[r]
    for step in range(1, height):
        copy, other = pe_copy(step)
        remote(pe.at[other], pe.at[other], pe_send, pe_recvs.at[other], (other, c)).wait_recv()
        summed = summed + pe[other]
    ps[c] = summed

    def ps_copy(step):
        other = lax.rem(c + step, breadth)
        return remote(ps.at[c], ps.at[c], ps_send, pt_recvs.at[c], (r, other)), other

    for step in range(1, breadth):
        ps_copy(step)[0].start()
    for s in range(2, breadth - 1):
        wr_pass(s)
    for step in range(2, height, 2):
        slot = lax.rem(r + step, height)
        wc_received(slot)
        wc_copy(slot, step + 1, mate).start()
    if breadth > 2:
        wr_pass(breadth - 1)
    projected = ps[c]
    for step in range(1, breadth):
        copy, other = ps_copy(step)
        remote(ps.at[other], ps.at[other], ps_send, pt_recvs.at[other], (r, other)).wait_recv()
        projected = projected + ps[other]

    projected = jnp.concatenate([projected[:, :B], projected[:, B:]], axis=0)
    factor = chained[:, :B]
    turned = factor.T
    inner = product(turned, product(projected, factor))
    upper, lower = split(jnp.concatenate([turned, -0.5 * inner], axis=1))
    mix = jnp.concatenate([upper, lower, upper], axis=1)
    wc_received(mate)
    for step in range(2, height, 2):
        wc_received(lax.rem(mate + step, height))
    for i in range(height):
        part = slice(i * width, (i + 1) * width)
        v = pc[i]
        u = product_halves(mix, jnp.concatenate([wc[i], v], axis=0))
        upper, lower = split(jnp.concatenate([u, v], axis=0))
        right[: 2 * B, part] = upper
        right[2 * B : 4 * B, part] = upper
        right[4 * B :, part] = lower

    @pl.when(c == reach)
    def _():
        for k in range(breadth):
            pl.when(k != c)(lambda: line_received(k))

    @pl.when(c < reach)
    def _():
        for k in range(breadth):
            line_copy(k).wait_send()

    @pl.when(root)
    def _():
        lower_top(pr)

    @pl.when(jnp.logical_not(jnp.logical_and(takes_left, takes_right)))
    def _():
        for k in range(breadth):

            @pl.when(k != c)
            def _():
                wr[k] = wc[lax.rem(r * breadth + k, height)]

    for i in range(breadth):
        part = slice(i * width, (i + 1) * width)
        v = pr[i]
        u = product_halves(mix, jnp.concatenate([wr[i], v], axis=0))
        upper, lower = split(jnp.concatenate([v, u], axis=0).T)
        left[part, : 2 * B] = upper
        left[part, 2 * B : 4 * B] = lower
        left[part, 4 * B :] = upper
    for index in range(breadth - 1):
        k, adds = chunk_at(index)
        if adds is None:
            raw_copy(index, k).wait_send()
        else:
            pl.when(adds)(sum_of_pair(index, k).wait_send)
            pl.when(jnp.logical_not(adds))(raw_copy(index, k).wait_send)

    @pl.when(root)
    def _():
        remote(parts, parts, part_send, part_recvs.at[0], (1, c)).wait_send()

    @pl.when(r == 1)
    def _():
        for q in range(1, half):
            stat_copy(q).wait_send()

    pl.when(odd)(chain_copy.wait_send)
    several = ps.at[pl.ds(0, breadth - 1)]
    remote(several, several, ps_send, pt_recvs.at[0], (mate, c)).wait_send()
    several = pe.at[pl.ds(0, height - 1)]
    remote(several, several, pe_send, pe_recvs.at[0], (mate, c)).wait_send()
    pl.when(jnp.logical_not(itself))(role.wait_send)
    several = wc.at[pl.ds(0, height - 1)]
    remote(several, several, wc_send, wc_recvs.at[0], (mate, c)).wait_send()

    @pl.when(has_right)
    def _():
        for k in range(breadth):
            pl.when(k <= c)(lambda: sum_sent(k, wr_right))

    @pl.when(has_left)
    def _():
        for k in range(breadth):
            pl.when(k >= c)(lambda: sum_sent(k, wr_left))


def front(matrix, height, breadth):
    rows, cols = matrix.shape
    width = cols // height
    vmem = pl.BlockSpec(memory_space=pltpu.VMEM)
    dma = pltpu.SemaphoreType.DMA
    scratch = [
        pltpu.VMEM((B, cols), f32),
        pltpu.VMEM((rows, 2 * B), f32),
        pltpu.VMEM((height, B, width), f32),
        pltpu.VMEM((breadth, B, width), f32),
        pltpu.VMEM((breadth, B, width), f32),
        pltpu.VMEM((2 * B, cols), bf16),
        pltpu.VMEM((B, 2 * B), f32),
        pltpu.VMEM((breadth, B, 2 * B), f32),
        pltpu.VMEM((B, 2 * B), f32),
        pltpu.VMEM((B, 2 * B), f32),
        pltpu.VMEM((breadth, B, width), f32),
        pltpu.VMEM((breadth, B, width), f32),
        pltpu.VMEM((breadth // 2, B, width), f32),
        pltpu.VMEM((height, B, width), f32),
        pltpu.VMEM((height, B // 2, 2 * B), f32),
        pltpu.VMEM((breadth, B // 2, 2 * B), f32),
        pltpu.VMEM((width, 2 * B), f32),
        dma((2,)),
        dma((breadth,)),
        dma((height, PIECES)),
        dma((2,)),
        dma((height,)),
        dma(()),
        dma((breadth,)),
        dma((breadth,)),
        dma(()),
        dma((breadth,)),
        dma((height // 2,)),
        dma(()),
        dma(()),
        dma(()),
        dma((breadth,)),
        dma((breadth,)),
        dma((breadth,)),
        dma((breadth // 2,)),
        dma((breadth,)),
        dma((breadth,)),
        dma((breadth, 2)),
        dma(()),
        dma((height,)),
        dma(()),
        dma(()),
        dma((height,)),
        dma(()),
        dma((breadth,)),
    ]
    return pl.pallas_call(
        lambda *refs: front_kernel(height, breadth, *refs),
        out_shape=[
            pltpu.VMEM((rows, cols), f32),
            pltpu.VMEM((rows, 6 * B), bf16),
            pltpu.VMEM((6 * B, cols), bf16),
        ],
        in_specs=[pl.BlockSpec(memory_space=pl.ANY)],
        out_specs=[vmem] * 3,
        scratch_shapes=scratch,
        compiler_params=pltpu.CompilerParams(
            collective_id=0, has_side_effects=True, vmem_limit_bytes=20 << 20
        ),
        name="front",
    )(matrix)


def final_kernel(tile, slots, block, left, right, out, buffer, sems, first_sems):
    rows, cols = block.shape
    size = min(512, cols)
    count = rows // tile

    def copy(i):
        return pltpu.make_async_copy(
            buffer.at[i % slots], out.at[pl.ds(i * tile, tile)], sems.at[i % slots]
        )

    def first_copy(at):
        part = pl.ds(at, size)
        return pltpu.make_async_copy(
            buffer.at[0, :, part], out.at[pl.ds(0, tile), part], first_sems.at[at // size]
        )

    def done(i):
        if i:
            copy(i).wait()
        else:
            for at in range(0, cols, size):
                first_copy(at).wait()

    for i in range(count):
        if i >= slots:
            done(i - slots)
        some = slice(i * tile, (i + 1) * tile)
        for at in range(0, cols, size):
            part = slice(at, at + size)
            buffer[i % slots, :, part] = block[some, part] - jnp.dot(
                left[some, :], right[:, part], preferred_element_type=f32
            )
            if not i:
                first_copy(at).start()
        if i:
            copy(i).start()
    for i in range(max(0, count - slots), count):
        done(i)


def final(block, left, right):
    rows, cols = block.shape
    tile = min(256, rows)
    slots = min(4, rows // tile)
    vmem = pl.BlockSpec(memory_space=pltpu.VMEM)
    held = [pltpu.with_memory_space_constraint(x, pltpu.VMEM) for x in (block, left, right)]
    return pl.pallas_call(
        lambda *refs: final_kernel(tile, slots, *refs),
        out_shape=jax.ShapeDtypeStruct((rows, cols), f32),
        in_specs=[vmem] * 3,
        out_specs=pl.BlockSpec(memory_space=pl.ANY),
        scratch_shapes=[
            pltpu.VMEM((slots, tile, cols), f32),
            pltpu.SemaphoreType.DMA((slots,)),
            pltpu.SemaphoreType.DMA((cols // min(512, cols),)),
        ],
        compiler_params=pltpu.CompilerParams(vmem_limit_bytes=20 << 20),
        name="final",
    )(*held)


def solution(mesh):
    height, breadth = mesh.shape["row"], mesh.shape["col"]

    def shards(matrix):
        return final(*front(matrix, height, breadth))

    return jax.shard_map(
        shards,
        mesh=mesh,
        in_specs=(P("row", "col"),),
        out_specs=P("row", "col"),
        check_vma=False,
    )
```

```python
import jax
import jax.numpy as jnp
from jax import lax
from jax.experimental import pallas as pl
from jax.experimental.pallas import tpu as pltpu
from jax.sharding import PartitionSpec as P

B = 64
STEP = 8
PIECES = 4


highest = lax.Precision.HIGHEST
MESH = pl.DeviceIdType.MESH
f32 = jnp.float32
bf16 = jnp.bfloat16
NT = (((1,), (1,)), ((), ()))
TN = (((0,), (0,)), ((), ()))


def product(left, right):
    return jnp.dot(left, right, precision=highest, preferred_element_type=f32)


def product_nt(left, right):
    return lax.dot_general(left, right, NT, precision=highest, preferred_element_type=f32)


def product_tn(left, right):
    return lax.dot_general(left, right, TN, precision=highest, preferred_element_type=f32)


def split(x):
    upper = x.astype(bf16)
    return upper, (x - upper.astype(f32)).astype(bf16)


def product_halves(left, right):
    upper, lower = split(right)
    return jnp.dot(left, jnp.concatenate([upper, upper, lower], axis=0), preferred_element_type=f32)


def eliminate(work, rows):
    for j in range(0, B, STEP):
        columns = [jnp.broadcast_to(work[:, j + k : j + k + 1], work.shape) for k in range(STEP)]
        lines = [work[j + k : j + k + 1, :] for k in range(STEP)]
        small = [[columns[c][j + r : j + r + 1, :] for c in range(STEP)] for r in range(STEP)]
        scaled = []
        for k in range(STEP):
            inverse = 1.0 / small[k][k]
            scaled.append(lines[k] * inverse)
            for m in range(k + 1, STEP):
                ratio = small[k][m] * inverse
                columns[m] = columns[m] - columns[k] * ratio
                lines[m] = lines[m] - lines[k] * ratio
                for c in range(m, STEP):
                    small[m][c] = small[m][c] - ratio * small[k][c]
        lowered = work
        for k in range(STEP):
            lowered = lowered - columns[k] * scaled[k]
        lowered = jnp.where(rows >= j + STEP, lowered, work)
        for k in range(1, STEP):
            lowered = jnp.where(rows == j + k, lines[k], lowered)
        work = lowered
    return work


def sign_inverse(q, rows):
    lane = lax.broadcasted_iota(jnp.int32, (1, 2 * B), 1)
    signs = jnp.zeros((B, 2 * B), f32)
    for j in range(0, B, STEP):
        columns = [jnp.broadcast_to(q[:, j + k : j + k + 1], q.shape) for k in range(STEP)]
        lines = [q[j + k : j + k + 1, :] for k in range(STEP)]
        small = [[columns[c][j + r : j + r + 1, :] for c in range(STEP)] for r in range(STEP)]
        scaled = []
        chosen = []
        for k in range(STEP):
            sign = jnp.where(small[k][k] >= 0, f32(-1.0), f32(1.0))
            pivot = small[k][k] - sign
            inverse = 1.0 / pivot
            chosen.append(sign)
            lines[k] = jnp.where(lane == j + k, pivot, lines[k]) * inverse
            scaled.append(lines[k])
            for c in range(k + 1, STEP):
                small[k][c] = small[k][c] * inverse
                columns[c] = columns[c] - columns[k] * small[k][c]
            for r in range(STEP):
                if r != k:
                    lines[r] = lines[r] - small[r][k] * lines[k]
                    for c in range(k + 1, STEP):
                        small[r][c] = small[r][c] - small[r][k] * small[k][c]
        for k in range(STEP):
            q = q - columns[k] * scaled[k]
        for k in range(STEP):
            q = jnp.where(rows == j + k, lines[k], q)
            signs = jnp.where(rows == j + k, chosen[k], signs)
    return q[:, B:], signs[:, :1]


def factor_values(gram, top):
    rows = lax.broadcasted_iota(jnp.int32, (B, 2 * B), 0)
    lanes = lax.broadcasted_iota(jnp.int32, (B, 2 * B), 1)
    small_rows = lax.broadcasted_iota(jnp.int32, (B, B), 0)
    small_lanes = lax.broadcasted_iota(jnp.int32, (B, B), 1)
    eye = jnp.where(small_rows == small_lanes, f32(1.0), f32(0.0))
    work = eliminate(jnp.concatenate([gram, eye], axis=1), rows)
    pivots = jnp.sum(jnp.where(rows == lanes, work, f32(0.0)), axis=1, keepdims=True)
    work = work * (1.0 / jnp.sqrt(pivots))
    upper = jnp.where(small_lanes >= small_rows, work[:, :B], f32(0.0))
    lower_inverse = work[:, B:]
    basis = product_nt(top, lower_inverse)
    inverse, signs = sign_inverse(jnp.concatenate([basis, eye], axis=1), rows)
    factor = -product_tn(lower_inverse, product(signs * inverse.T, lower_inverse))
    return factor, (signs * upper).T


def remote(src, dst, send_sem, recv_sem, device):
    return pltpu.make_async_remote_copy(
        src_ref=src,
        dst_ref=dst,
        send_sem=send_sem,
        recv_sem=recv_sem,
        device_id=device,
        device_id_type=MESH,
    )


def front_kernel(
    height, breadth, matrix, block, left, right,
    slab, strip, pc, pr, wr, halves, own, parts, stats, chained, zs, near, rs, wc, pe, ps, sums,
    local_sems, block_sems, pc_recvs, ring_far, ring_sends, mate_send, pr_recvs, pr_sends, part_send, part_recvs,
    stat_sends, stat_recv, chain_send, chain_recv, raw_sends, near_recvs, rs_sends, rs_recvs, wr_right, wr_left, wr_recvs,
    role_send, wc_recvs, wc_send, pe_send, pe_recvs, ps_send, pt_recvs,
):
    r, c = lax.axis_index("row"), lax.axis_index("col")
    rows, cols = matrix.shape
    width = cols // height
    half = height // 2
    count = height * breadth
    me = r * breadth + c
    core = lax.rem(r, 2)
    chip = r // 2
    even = core == 0
    odd = core == 1
    mate = r + 1 - 2 * core
    place = 2 * (chip // 2) + lax.rem(lax.rem(chip, 2) + chip // 2, 2)

    def seat(q):
        return 2 * (2 * (q // 2) + lax.rem(q + q // 2, 2))

    root = r == 0
    edge = c == 0
    home = r // (height // breadth)
    low_home = home == 0
    high_home = home == breadth - 1
    at_home = jnp.logical_and(high_home, c == breadth - 1)
    reach = jnp.where(high_home, breadth - 2, breadth - 1)

    pair = c // 2
    late = lax.rem(c, 2)
    friend = c + 1 - 2 * late
    pairs = breadth // 2

    def chunk_at(index):
        if index < breadth - 2:
            whose = lax.rem(pair + 1 + index // 2, pairs)
            above = jnp.where(whose > pair, 1, 0)
            first = jnp.where(whose > pair, 1 - index % 2, index % 2)
            return 2 * whose + first, above == late
        return (friend if index == breadth - 2 else c), None

    slab_copy = pltpu.make_async_copy(matrix.at[pl.ds(0, B)], slab, local_sems.at[0])
    strip_copy = pltpu.make_async_copy(matrix.at[:, pl.ds(0, 2 * B)], strip, local_sems.at[1])
    pl.when(root)(slab_copy.start)
    pl.when(edge)(strip_copy.start)
    def block_rows(index):
        k = chunk_at(index)[0]
        return pl.ds(pl.multiple_of(k * width, width), width)

    def block_copy(index):
        part = block_rows(index)
        return pltpu.make_async_copy(matrix.at[part], block.at[part], block_sems.at[index])

    sums[...] = jnp.zeros_like(sums)
    barrier = pltpu.get_barrier_semaphore()

    def greet(step, carry):
        other = lax.rem(me + step, count)
        pl.semaphore_signal(
            barrier, inc=1, device_id=(other // breadth, lax.rem(other, breadth)), device_id_type=MESH
        )
        return carry

    lax.fori_loop(1, count, greet, 0)

    def masked_slab():
        lane = lax.broadcasted_iota(jnp.int32, (B, cols), 1) + c * cols
        return jnp.where(lane >= B, slab[...], f32(0.0))

    @pl.when(root)
    def _():
        slab_copy.wait()
        panel = masked_slab()
        for i in range(height):
            pc[i] = panel[:, i * width : (i + 1) * width]

    pl.when(edge)(strip_copy.wait)
    for index in range(breadth):
        block_copy(index).start()

    @pl.when(root)
    def _():
        panel = masked_slab()
        top = jnp.where(edge, slab[:, B : 2 * B], f32(0.0))
        own[...] = jnp.concatenate([product_nt(panel, panel), top], axis=1)

    @pl.when(edge)
    def _():
        for k in range(breadth):
            piece = strip[k * width : (k + 1) * width, :].T[:B, :]
            lane = lax.broadcasted_iota(jnp.int32, (B, width), 1) + r * rows + k * width
            pr[k] = jnp.where(lane >= B, piece, f32(0.0))

    pl.semaphore_wait(barrier, count - 1)

    def piece_copy(i, part, send, target):
        some = pc.at[i, pl.ds(part * (B // PIECES), B // PIECES)]
        return remote(some, some, send, pc_recvs.at[i, part], (target, c))

    def ring_copy(i, part, target):
        return piece_copy(i, part, ring_sends.at[i], target)

    def mate_copy(i, part):
        return piece_copy(i, part, mate_send, mate)

    def chunk_sent(i, send):
        remote(pc.at[i], pc.at[i], send, pc_recvs.at[i, 0], (mate, c)).wait_send()

    def all_sent(send):
        remote(pc, pc, send, pc_recvs.at[0, 0], (mate, c)).wait_send()

    def part_copy(k):
        return remote(own, parts.at[c], part_send, part_recvs.at[c], (1, k))

    forth = seat(lax.rem(place + 1, half))
    back = seat(lax.rem(place + half - 1, half))
    straight = half > 2

    def goes(i):
        short = 1 if straight and i % half == half - 1 else 0
        return place + 1 < half - short if i < half else place > 1 + short

    def straight_copy(i, part):
        return piece_copy(i, part, ring_far.at[i // half], back if i < half else forth)

    def ring_on(i, part):
        pl.when(goes(i))(ring_copy(i, part, forth if i < half else back).start)

    def passed(i, part):
        mate_copy(i, part).wait_recv()
        ring_on(i, part)
        mate_copy(i, part).start()

    @pl.when(root)
    def _():
        for k in range(breadth):
            part_copy(k).start()
        for i in range(half):
            for part in range(PIECES):
                ring_copy(i, part, forth).start()
                ring_copy(half + i, part, back).start()
        for part in range(PIECES if straight else 0):
            straight_copy(half - 1, part).start()
            straight_copy(height - 1, part).start()

    def line_copy(k):
        return remote(pr.at[k], pr.at[k], pr_sends.at[k], pr_recvs.at[k], (r, c + 1))

    def line_received(k):
        remote(pr.at[k], pr.at[k], pr_sends.at[k], pr_recvs.at[k], (r, 0)).wait_recv()

    @pl.when(edge)
    def _():
        for k in range(breadth - 1, -1, -1):
            line_copy(k).start()

    middle = jnp.logical_and(c >= 1, c < reach)

    def line_pass(who, index, when=True):
        k = breadth - 1 - index

        @pl.when(jnp.logical_and(jnp.logical_and(middle, c == who), when))
        def _():
            line_received(k)
            line_copy(k).start()

    relays = jnp.logical_and(even, jnp.logical_not(root))

    def share(some, part):
        upper, lower = split(block[some, part])
        both = lax.dot_general(upper, halves[:, part], NT, preferred_element_type=f32)
        low = lax.dot_general(lower, halves[:, part], NT, preferred_element_type=f32)
        return both + jnp.where(lax.broadcasted_iota(jnp.int32, both.shape, 1) < B, low, f32(0.0))

    topmost = [i for i in range(height) if max(B, i * width) < min(2 * B, (i + 1) * width)]

    def halve(i):
        some = slice(i * width, (i + 1) * width)
        upper, lower = split(pc[i])
        halves[:B, some] = upper
        halves[B:, some] = lower
        if i not in topmost:
            sums[...] = sums[...] + share(block_rows(0), some)

    block_copy(0).wait()

    def go_round(pieces):
        for step, (i, part) in enumerate(pieces):
            passed(i, part)
            if part == PIECES - 1:
                halve(i)
            for index in range(breadth):
                if (index + 1) * len(pieces) // breadth - 1 == step:
                    line_pass(1, index)

    pieces = [(i, part) for i in range(height) for part in range(PIECES)]
    turn = len(pieces) // 2
    later = pieces[turn:] + pieces[:turn]

    @pl.when(jnp.logical_and(relays, 2 * place < half))
    def _():
        go_round(pieces)

    @pl.when(jnp.logical_and(relays, 2 * place == half))
    def _():
        go_round([piece for pair in zip(pieces[:turn], later[:turn]) for piece in pair])

    @pl.when(jnp.logical_and(relays, 2 * place > half))
    def _():
        go_round(later)

    @pl.when(root)
    def _():
        for i in range(height):
            chunk_sent(i, ring_sends.at[i])
        if straight:
            chunk_sent(half - 1, ring_far.at[0])
            chunk_sent(height - 1, ring_far.at[1])
        for i, part in pieces:
            mate_copy(i, part).start()
        for i in range(height):
            halve(i)
        for index in range(breadth):
            line_pass(1, index)

    def stat_copy(q):
        return remote(stats, stats, stat_sends.at[q], stat_recv, (2 * q + 1, c))

    chain_copy = remote(chained, chained, chain_send, chain_recv, (mate, c))

    @pl.when(r == 1)
    def _():
        total = None
        for k in range(breadth):
            remote(parts.at[k], parts.at[k], part_send, part_recvs.at[k], (0, c)).wait_recv()
            total = parts[k] if total is None else total + parts[k]
        stats[...] = total
        for q in range(1, half):
            stat_copy(q).start()

    pl.when(odd)(lambda: line_pass(1, 0))

    @pl.when(jnp.logical_and(odd, r != 1))
    def _():
        remote(stats, stats, stat_sends.at[0], stat_recv, (1, c)).wait_recv()

    @pl.when(odd)
    def _():
        factor, turned = factor_values(stats[:, :B], stats[:, B:].T)
        chained[...] = jnp.concatenate([factor, turned], axis=1)
        chain_copy.start()
        for index in range(1, breadth):
            line_pass(1, index)
        for i, part in pieces:
            mate_copy(i, part).wait_recv()
            if part == PIECES - 1:
                halve(i)

    @pl.when(even)
    def _():
        all_sent(mate_send)
        chain_copy.wait_recv()

    @pl.when(relays)
    def _():
        for i in range(height):
            pl.when(goes(i))(lambda: chunk_sent(i, ring_sends.at[i]))

    def lower_top(buffer):
        for i in range(buffer.shape[0]):
            low, high = max(B, i * width), min(2 * B, (i + 1) * width)
            if low < high:
                lanes = slice(low - i * width, high - i * width)
                buffer[i, :, lanes] = buffer[i, :, lanes] - chained[:, low : high]

    @pl.when(edge)
    def _():
        lower_top(pc)
        for i in topmost:
            halve(i)

    @pl.when(at_home)
    def _():
        for k in range(breadth):
            pr[k] = pc[lax.rem(r * breadth + k, height)]

    for index in range(1, breadth):
        block_copy(index).wait()

    size = min(512, cols)

    def raw_copy(index, k):
        return remote(zs.at[k], near.at[k], raw_sends.at[index], near_recvs.at[k], (r, friend))

    def sum_of_pair(index, k):
        return remote(zs.at[k], rs.at[pair], rs_sends.at[index], rs_recvs.at[pair], (r, k))

    def add_pair(index):
        k, adds = chunk_at(index)

        @pl.when(adds)
        def _():
            raw_copy(index, k).wait_recv()
            zs[k] = zs[k] + near[k]
            sum_of_pair(index, k).start()

    for index in range(breadth):
        if index in (0, breadth // 2):
            for k in range(breadth // 2):
                line_pass(2, k, (r >= 2) if index == 0 else (r < 2))
        other, adds = chunk_at(index)
        some = block_rows(index)
        if index == 0:
            both = sums[...]
            for i in topmost:
                both = both + share(some, slice(i * width, (i + 1) * width))
        else:
            both = jnp.zeros((width, 2 * B), f32)
            for start in range(0, cols, size):
                both = both + share(some, slice(start, start + size))
        turned = both.T
        value = turned[:B, :] + turned[B:, :]
        zs[other] = value
        if index < breadth - 2:
            pl.when(jnp.logical_not(adds))(raw_copy(index, other).start)
        elif index == breadth - 2:
            raw_copy(index, other).start()
        if index >= 2:
            add_pair(index - 2)
    for k in range(breadth // 2, breadth):
        line_pass(2, k)
    for who in range(3, breadth - 1):
        for k in range(breadth):
            line_pass(who, k)

    raw_copy(0, c).wait_recv()
    total = zs[c] + near[c]
    for step in range(1, pairs):
        other = lax.rem(pair + step, pairs)
        remote(rs.at[other], rs.at[other], rs_sends.at[0], rs_recvs.at[other], (r, friend)).wait_recv()
        total = total + rs[other]
    wr[c] = total

    def sum_copy(k, part, sends, target):
        some = wr.at[k, pl.ds(part * (B // 2), B // 2)]
        return remote(some, some, sends.at[k], wr_recvs.at[k, part], (r, target))

    def sum_sent(k, sends):
        remote(wr.at[k], wr.at[k], sends.at[k], wr_recvs.at[k, 0], (r, c)).wait_send()

    def right_copy(k, part):
        return sum_copy(k, part, wr_right, c + 1)

    def left_copy(k, part):
        return sum_copy(k, part, wr_left, c - 1)

    has_right = jnp.logical_and(c + 1 < breadth, jnp.logical_not(jnp.logical_and(high_home, c == breadth - 2)))
    has_left = jnp.logical_and(c >= 1, jnp.logical_not(jnp.logical_and(low_home, c == 1)))
    takes_right = jnp.logical_not(jnp.logical_and(low_home, edge))
    takes_left = jnp.logical_not(jnp.logical_and(high_home, c == breadth - 1))
    to_row = lax.rem(me, height)
    to_col = me // height
    itself = jnp.logical_and(to_row == r, to_col == c)
    role = remote(wr.at[c], wc.at[to_row], role_send, wc_recvs.at[to_row], (to_row, to_col))
    pl.when(jnp.logical_not(itself))(role.start)
    for part in range(2):
        pl.when(has_right)(right_copy(c, part).start)
        pl.when(has_left)(left_copy(c, part).start)

    @pl.when(itself)
    def _():
        wc[r] = total

    @pl.when(c == reach)
    def _():
        line_received(c)

    slots = lax.broadcasted_iota(jnp.int32, (B, width), 0)
    positions = lax.broadcasted_iota(jnp.int32, (B, width), 1) + me * width - B
    onehot = jnp.where(positions == slots, f32(1.0), f32(0.0))
    vector = pr[c] - product(chained[:, B:], onehot)
    part_of = product_nt(total, vector)
    pe[r] = jnp.concatenate([part_of[: B // 2], part_of[B // 2 :]], axis=1)

    def pe_copy(step):
        other = lax.rem(r + step, height)
        return remote(pe.at[r], pe.at[r], pe_send, pe_recvs.at[r], (other, c)), other

    for step in range(1, height):
        pe_copy(step)[0].start()

    def wr_pass(s):
        for part in range(2):

            @pl.when(jnp.logical_and(c - s >= 0, takes_left))
            def _():
                sum_copy(c - s, part, wr_right, c - 1).wait_recv()
                pl.when(has_right)(right_copy(c - s, part).start)

            @pl.when(jnp.logical_and(c + s < breadth, takes_right))
            def _():
                sum_copy(c + s, part, wr_left, c + 1).wait_recv()
                pl.when(has_left)(left_copy(c + s, part).start)

    def wc_copy(slot, step, other):
        return remote(wc.at[slot], wc.at[slot], wc_send, wc_recvs.at[slot], (other, c))

    def wc_received(slot):
        remote(wc.at[slot], wc.at[slot], wc_send, wc_recvs.at[slot], (mate, c)).wait_recv()

    pl.when(jnp.logical_not(itself))(lambda: wc_received(r))
    for step in range(2, height, 2):
        wc_copy(r, step, lax.rem(r + step, height)).start()
    wc_copy(r, 1, mate).start()
    wr_pass(1)
    summed = pe[r]
    for step in range(1, height):
        copy, other = pe_copy(step)
        remote(pe.at[other], pe.at[other], pe_send, pe_recvs.at[other], (other, c)).wait_recv()
        summed = summed + pe[other]
    ps[c] = summed

    def ps_copy(step):
        other = lax.rem(c + step, breadth)
        return remote(ps.at[c], ps.at[c], ps_send, pt_recvs.at[c], (r, other)), other

    for step in range(1, breadth):
        ps_copy(step)[0].start()
    for s in range(2, breadth - 1):
        wr_pass(s)
    for step in range(2, height, 2):
        slot = lax.rem(r + step, height)
        wc_received(slot)
        wc_copy(slot, step + 1, mate).start()
    if breadth > 2:
        wr_pass(breadth - 1)
    projected = ps[c]
    for step in range(1, breadth):
        copy, other = ps_copy(step)
        remote(ps.at[other], ps.at[other], ps_send, pt_recvs.at[other], (r, other)).wait_recv()
        projected = projected + ps[other]

    projected = jnp.concatenate([projected[:, :B], projected[:, B:]], axis=0)
    factor = chained[:, :B]
    turned = factor.T
    inner = product(turned, product(projected, factor))
    upper, lower = split(jnp.concatenate([turned, -0.5 * inner], axis=1))
    mix = jnp.concatenate([upper, lower, upper], axis=1)
    wc_received(mate)
    for step in range(2, height, 2):
        wc_received(lax.rem(mate + step, height))
    for i in range(height):
        part = slice(i * width, (i + 1) * width)
        v = pc[i]
        u = product_halves(mix, jnp.concatenate([wc[i], v], axis=0))
        upper, lower = split(jnp.concatenate([u, v], axis=0))
        right[: 2 * B, part] = upper
        right[2 * B : 4 * B, part] = upper
        right[4 * B :, part] = lower

    @pl.when(c == reach)
    def _():
        for k in range(breadth):
            pl.when(k != c)(lambda: line_received(k))

    @pl.when(c < reach)
    def _():
        for k in range(breadth):
            line_copy(k).wait_send()

    @pl.when(root)
    def _():
        lower_top(pr)

    @pl.when(jnp.logical_not(jnp.logical_and(takes_left, takes_right)))
    def _():
        for k in range(breadth):

            @pl.when(k != c)
            def _():
                wr[k] = wc[lax.rem(r * breadth + k, height)]

    for i in range(breadth):
        part = slice(i * width, (i + 1) * width)
        v = pr[i]
        u = product_halves(mix, jnp.concatenate([wr[i], v], axis=0))
        upper, lower = split(jnp.concatenate([v, u], axis=0).T)
        left[part, : 2 * B] = upper
        left[part, 2 * B : 4 * B] = lower
        left[part, 4 * B :] = upper
    for index in range(breadth - 1):
        k, adds = chunk_at(index)
        if adds is None:
            raw_copy(index, k).wait_send()
        else:
            pl.when(adds)(sum_of_pair(index, k).wait_send)
            pl.when(jnp.logical_not(adds))(raw_copy(index, k).wait_send)

    @pl.when(root)
    def _():
        remote(parts, parts, part_send, part_recvs.at[0], (1, c)).wait_send()

    @pl.when(r == 1)
    def _():
        for q in range(1, half):
            stat_copy(q).wait_send()

    pl.when(odd)(chain_copy.wait_send)
    several = ps.at[pl.ds(0, breadth - 1)]
    remote(several, several, ps_send, pt_recvs.at[0], (mate, c)).wait_send()
    several = pe.at[pl.ds(0, height - 1)]
    remote(several, several, pe_send, pe_recvs.at[0], (mate, c)).wait_send()
    pl.when(jnp.logical_not(itself))(role.wait_send)
    several = wc.at[pl.ds(0, height - 1)]
    remote(several, several, wc_send, wc_recvs.at[0], (mate, c)).wait_send()

    @pl.when(has_right)
    def _():
        for k in range(breadth):
            pl.when(k <= c)(lambda: sum_sent(k, wr_right))

    @pl.when(has_left)
    def _():
        for k in range(breadth):
            pl.when(k >= c)(lambda: sum_sent(k, wr_left))


def front(matrix, height, breadth):
    rows, cols = matrix.shape
    width = cols // height
    vmem = pl.BlockSpec(memory_space=pltpu.VMEM)
    dma = pltpu.SemaphoreType.DMA
    scratch = [
        pltpu.VMEM((B, cols), f32),
        pltpu.VMEM((rows, 2 * B), f32),
        pltpu.VMEM((height, B, width), f32),
        pltpu.VMEM((breadth, B, width), f32),
        pltpu.VMEM((breadth, B, width), f32),
        pltpu.VMEM((2 * B, cols), bf16),
        pltpu.VMEM((B, 2 * B), f32),
        pltpu.VMEM((breadth, B, 2 * B), f32),
        pltpu.VMEM((B, 2 * B), f32),
        pltpu.VMEM((B, 2 * B), f32),
        pltpu.VMEM((breadth, B, width), f32),
        pltpu.VMEM((breadth, B, width), f32),
        pltpu.VMEM((breadth // 2, B, width), f32),
        pltpu.VMEM((height, B, width), f32),
        pltpu.VMEM((height, B // 2, 2 * B), f32),
        pltpu.VMEM((breadth, B // 2, 2 * B), f32),
        pltpu.VMEM((width, 2 * B), f32),
        dma((2,)),
        dma((breadth,)),
        dma((height, PIECES)),
        dma((2,)),
        dma((height,)),
        dma(()),
        dma((breadth,)),
        dma((breadth,)),
        dma(()),
        dma((breadth,)),
        dma((height // 2,)),
        dma(()),
        dma(()),
        dma(()),
        dma((breadth,)),
        dma((breadth,)),
        dma((breadth,)),
        dma((breadth // 2,)),
        dma((breadth,)),
        dma((breadth,)),
        dma((breadth, 2)),
        dma(()),
        dma((height,)),
        dma(()),
        dma(()),
        dma((height,)),
        dma(()),
        dma((breadth,)),
    ]
    return pl.pallas_call(
        lambda *refs: front_kernel(height, breadth, *refs),
        out_shape=[
            pltpu.VMEM((rows, cols), f32),
            pltpu.VMEM((rows, 6 * B), bf16),
            pltpu.VMEM((6 * B, cols), bf16),
        ],
        in_specs=[pl.BlockSpec(memory_space=pl.ANY)],
        out_specs=[vmem] * 3,
        scratch_shapes=scratch,
        compiler_params=pltpu.CompilerParams(
            collective_id=0, has_side_effects=True, vmem_limit_bytes=20 << 20
        ),
        name="front",
    )(matrix)


def final_kernel(tile, slots, size, block, left, right, out, buffer, sems):
    rows, cols = block.shape
    count = rows // tile

    def copy(i, at):
        part = pl.ds(at, size)
        return pltpu.make_async_copy(
            buffer.at[i % slots, :, part],
            out.at[pl.ds(i * tile, tile), part],
            sems.at[i % slots, at // size],
        )

    def done(i):
        for at in range(0, cols, size):
            copy(i, at).wait()

    for i in range(count):
        if i >= slots:
            done(i - slots)
        some = slice(i * tile, (i + 1) * tile)
        for at in range(0, cols, size):
            part = slice(at, at + size)
            buffer[i % slots, :, part] = block[some, part] - jnp.dot(
                left[some, :], right[:, part], preferred_element_type=f32
            )
            copy(i, at).start()
    for i in range(max(0, count - slots), count):
        done(i)


def final(block, left, right):
    rows, cols = block.shape
    tile = min(256, rows)
    slots = min(4, rows // tile)
    size = min(512, cols)
    vmem = pl.BlockSpec(memory_space=pltpu.VMEM)
    held = [pltpu.with_memory_space_constraint(x, pltpu.VMEM) for x in (block, left, right)]
    return pl.pallas_call(
        lambda *refs: final_kernel(tile, slots, size, *refs),
        out_shape=jax.ShapeDtypeStruct((rows, cols), f32),
        in_specs=[vmem] * 3,
        out_specs=pl.BlockSpec(memory_space=pl.ANY),
        scratch_shapes=[
            pltpu.VMEM((slots, tile, cols), f32),
            pltpu.SemaphoreType.DMA((slots, cols // size)),
        ],
        compiler_params=pltpu.CompilerParams(vmem_limit_bytes=20 << 20),
        name="final",
    )(*held)


def solution(mesh):
    height, breadth = mesh.shape["row"], mesh.shape["col"]

    def shards(matrix):
        return final(*front(matrix, height, breadth))

    return jax.shard_map(
        shards,
        mesh=mesh,
        in_specs=(P("row", "col"),),
        out_specs=P("row", "col"),
        check_vma=False,
    )
```
